32 devices in a mesh: tm: 8 (over z, y), swath: 4 (over x, core).
Axes of the slice: x: 2, y: 2, z: 4, core: 2. Of those that a mesh axis runs over, the one named last changes fastest.
Arguments:
- design: bfloat16 [8, 2048, 512], P('tm', 'swath'), may hold values from -6 to 6
- process: bfloat16 [8, 512, 512], P('tm', 'swath')
- prior_prec: float32 [8, 512], P('tm', 'swath'), may hold values from 0.05 to 0.5
- routes: int32 [8, 16], P('tm', 'swath'), may hold values from -1 to 7, as said below
- counts: int32 [8, 4], P('tm', 'swath'), may hold values from 1 to 4
Outputs:
- reduced_diag: float32 [8, 512, 512], P('tm', 'swath')
- reduced_coupling: float32 [8, 512, 512], P('tm', 'swath')
The draws below stay inside these ranges and needn't reach their ends.
Inputs may be any that keep to these rules, and one draw needn't show every extreme that they name: `routes`: each value is the holder's own time block i or i + 1, or -1 only where i + 1 would be 8; of one holder's 4 blocks, exactly 2 name i and the others i + 1 or -1.
All inputs are finite; a program needn't handle non-finite values.
Results may differ from the reference program's by a relative error of at most 0.00073.
Values may be sent and summed in bfloat16 or wider, within the bound.
A program may use at most 64 MiB of HBM per device.

```python
import math
import jax
import jax.numpy as jnp
from jax import lax

B = 512
OBS = 128
CAP = 2
LEVELS = 3
RB = 4
NT = 8
SLOTS = 2048
N_SWATH = 4


def draw_process(key, part):
    first_key, second_key = jax.random.split(jax.random.fold_in(key, 7))
    base = jnp.exp(jax.random.uniform(first_key, (NT, B), jnp.float32, math.log(0.2), math.log(2.0)))
    noise = jax.random.normal(second_key, (NT, B, B), jnp.float32)
    outer = jnp.einsum('tij,tkj->tik', noise, noise, precision=lax.Precision.HIGHEST) / (2.0 * B)
    outer = 0.5 * (outer + jnp.swapaxes(outer, 1, 2))
    matrix = outer + base[:, :, None] * jnp.eye(B, dtype=jnp.float32)[None]
    return matrix.astype(jnp.bfloat16)


def draw_routes(key, part):
    score_key = jax.random.fold_in(key, 11)
    scores = jax.random.randint(score_key, (NT, N_SWATH, RB), 0, 1048576) * RB + jnp.arange(RB, dtype=jnp.int32)
    ranking = jnp.argsort(jnp.argsort(scores, axis=-1), axis=-1)
    ahead = (ranking >= CAP).astype(jnp.int32)
    target = jnp.arange(NT, dtype=jnp.int32)[:, None, None] + ahead
    target = jnp.where(target > NT - 1, -1, target)
    return target.reshape(NT, N_SWATH * RB).astype(jnp.int32)


def draw_counts(key, part):
    first_key, second_key, third_key = jax.random.split(jax.random.fold_in(key, 3), 3)
    values = jax.random.randint(first_key, (NT, N_SWATH), 1, RB + 1)
    row_pick = jax.random.randint(second_key, (), 1, NT)
    col_pick = jax.random.randint(third_key, (), 0, N_SWATH)
    values = values.at[row_pick, col_pick].set(RB)
    values = values.at[row_pick - 1, col_pick].set(RB)
    values = values.at[(row_pick + 1) % NT, col_pick].set(1)
    return values.astype(jnp.int32)


def block_levels(rng, extent, cuts, smallest, largest):
    def one(position, blocks):
        draws = jax.random.uniform(jax.random.fold_in(jax.random.fold_in(rng, 6), position), (blocks,), jnp.float32, smallest / len(cuts), largest / len(cuts))
        return jnp.repeat(jnp.exp(draws), extent[position] // blocks).reshape((-1,) + (1,) * (len(extent) - position - 1))

    factor_of = one(*cuts[0])
    for cut in cuts[1:]:
        factor_of = factor_of * one(*cut)
    return factor_of


def normal_values(own_key, dims, width, most, cuts=(), held_as=jnp.bfloat16):
    result = jax.random.normal(own_key, dims, jnp.float32) * width
    if len(cuts) > 0:
        result = block_levels(own_key, dims, cuts, -0.22, 0.18) * result
    return jnp.clip(result, min=-most, max=most).astype(held_as)


def setup_inputs(seed: int = 0) -> dict:
    seeds = jax.random.split(jax.random.key(seed), 6)
    design = normal_values(seeds[0], (NT, N_SWATH * RB * OBS, B), 1.0, 6.0, ((0, 8), (1, 4)))
    process = draw_process(jax.random.fold_in(seeds[5], 71), 0)
    prior_prec = jnp.clip(jnp.exp(math.log(0.5) - 2.3025851 * jax.random.uniform(seeds[2], (NT, B), jnp.float32) ** block_levels(seeds[2], (NT, B), ((0, 8), (1, 4)), -0.2, 0.2)), 0.05, 0.5)
    routes = draw_routes(jax.random.fold_in(seeds[5], 71), 0)
    counts = draw_counts(jax.random.fold_in(seeds[5], 71), 0)
    return dict(design=design, process=process, prior_prec=prior_prec, routes=routes, counts=counts)


def tri_solve(factor, right):
    return lax.linalg.triangular_solve(factor, right, left_side=True, lower=True)

def reference(design, process, prior_prec, routes, counts):
    raw_rows = design.astype(jnp.float32).reshape(NT, N_SWATH, RB, OBS, B)
    mean_sq = lax.optimization_barrier(jnp.mean(raw_rows * raw_rows, axis=-1, keepdims=True))
    scaled = raw_rows * lax.rsqrt(4.0 * SLOTS * (mean_sq + 1e-06))
    live = jnp.arange(RB)[None, None, :] < counts[:, :, None]
    target = routes.reshape(NT, N_SWATH, RB)
    time_ids = jnp.arange(NT)[:, None, None]
    to_self = live & (target == time_ids)
    to_next = live & (target == time_ids + 1)
    self_rows = jnp.where(to_self[:, :, :, None, None], scaled, 0.0).astype(jnp.bfloat16)
    next_rows = jnp.where(to_next[:, :, :, None, None], scaled, 0.0).astype(jnp.bfloat16)

    def holder_grams(pair):
        own_rows, ahead_rows = pair
        own_rows = own_rows.reshape(-1, B)
        ahead_rows = ahead_rows.reshape(-1, B)
        own_gram = lax.dot_general(own_rows.astype(jnp.float32), own_rows.astype(jnp.float32), (((0,), (0,)), ((), ())), preferred_element_type=jnp.float32)
        ahead_gram = lax.dot_general(ahead_rows.astype(jnp.float32), ahead_rows.astype(jnp.float32), (((0,), (0,)), ((), ())), preferred_element_type=jnp.float32)
        return (own_gram, ahead_gram)
    gram_self, gram_next = lax.map(holder_grams, (self_rows, next_rows))
    zero_block = jnp.zeros((1, B, B), jnp.float32)
    gram = gram_self + jnp.concatenate([zero_block, gram_next[:-1]], axis=0)
    proc = process.astype(jnp.float32)
    previous = jnp.concatenate([zero_block, proc[:-1]], axis=0)
    unit = jnp.eye(B, dtype=jnp.float32)
    diag_blocks = previous + proc + gram + prior_prec[:, :, None] * unit[None]
    coupling = -proc
    for level in range(LEVELS):
        distance = 2 ** level
        factor = jnp.linalg.cholesky(diag_blocks)
        solved = tri_solve(factor, coupling)
        eliminated = jnp.einsum('tji,tjk->tik', solved, solved, precision=lax.Precision.HIGHEST)
        zero_run = jnp.zeros((distance, B, B), jnp.float32)
        left_term = jnp.concatenate([zero_run, eliminated[:-distance]], axis=0)
        unit_run = jnp.broadcast_to(unit, (distance, B, B))
        far_factor = jnp.concatenate([factor[distance:], unit_run], axis=0)
        far_solved = jnp.concatenate([solved[distance:], zero_run], axis=0)
        has_partner = (jnp.arange(NT) + distance < NT)[:, None, None]
        cross = tri_solve(far_factor, jnp.swapaxes(coupling, 1, 2))
        right_term = jnp.einsum('tji,tjk->tik', cross, cross, precision=lax.Precision.HIGHEST)
        new_coupling = jnp.einsum('tji,tjk->tik', cross, far_solved, precision=lax.Precision.HIGHEST)
        diag_blocks = diag_blocks - left_term - jnp.where(has_partner, right_term, 0.0)
        coupling = -new_coupling
    return (diag_blocks, coupling)
```

```python
import functools

import jax
import jax.numpy as jnp
from jax import lax
from jax.experimental import pallas as pl
from jax.experimental.pallas import tpu as pltpu
from jax.sharding import PartitionSpec as P

LEVELS = 3
PIECES = 4
W = 8


def split(x):
    high = x.astype(jnp.bfloat16)
    return high, (x - high.astype(jnp.float32)).astype(jnp.bfloat16)


def dot3(a, b, left):
    (ah, al), (bh, bl) = a, b
    dot = functools.partial(
        lax.dot_general,
        dimension_numbers=(((left,), (0,)), ((), ())),
        preferred_element_type=jnp.float32,
    )
    return dot(ah, bh) + (dot(ah, bl) + dot(al, bh))


def joined(a, b, dims):
    (ah, al), (bh, bl) = a, b
    return lax.dot_general(
        jnp.concatenate([ah, ah, al], axis=dims[0]),
        jnp.concatenate([bh, bl, bh], axis=dims[1]),
        (((dims[0],), (dims[1],)), ((), ())),
        preferred_element_type=jnp.float32,
    )

def pivots(columns):
    spread = lambda x: jnp.broadcast_to(x, columns[0].shape)
    entry = {(k, s): spread(columns[s][k : k + 1, :]) for s in range(W) for k in range(s, W)}
    scale, lower = [], {}
    for s in range(W):
        pivot = entry[s, s]
        turned = 1.0 / pivot
        scale.append(lax.rsqrt(pivot))
        if s + 1 < W:
            near = entry[s + 1, s]
            entry[s + 1, s + 1] = entry[s + 1, s + 1] - (near * near) * turned
        for k in range(s + 1, W):
            lower[k, s] = entry[k, s] * scale[s]
        for k in range(s + 2, W):
            part = entry[k, s] * turned
            for t in range(s + 1, k + 1):
                entry[k, t] = entry[k, t] - part * entry[t, s]
    return scale, lower

def forward(values, scale, lower):
    out = []
    values = list(values)
    for s in range(W):
        out.append(values[s] * scale[s])
        for k in range(s + 1, W):
            values[k] = values[k] - lower[k, s] * out[s]
    return out

def factor_inverse(m, panel=32):
    n = m.shape[0]
    rows = [m[W * g : W * (g + 1), :] for g in range(n // W)]
    lane = lax.broadcasted_iota(jnp.int32, (W, n), 1)
    sub = lax.broadcasted_iota(jnp.int32, (W, n), 0)
    spread = lambda x: jnp.broadcast_to(x, (W, n))
    cleared = lambda x, first: jnp.where((lane >= first) & (lane < first + W), 0.0, x)
    column = lambda h, first: [spread(rows[h][:, first + s : first + s + 1]) for s in range(W)]

    def solve_rows(row, first, scale, lower):
        row = cleared(row, first)
        start = [jnp.where(lane == first + s, 1.0, spread(row[s : s + 1, :])) for s in range(W)]
        solved = forward(start, scale, lower)
        group = solved[0]
        for s in range(1, W):
            group = jnp.where(sub == s, solved[s], group)
        return solved, group

    def take(row, factors, solved, first):
        row = cleared(row, first)
        for s in range(W):
            row = row - factors[s] * solved[s]
        return row

    per = panel // W
    for p in range(n // panel):
        end = (p + 1) * per
        for q in range(0, per, 2):
            g, h = p * per + q, p * per + q + 1
            first, second = g * W, h * W
            scale, lower = pivots(column(g, first))
            cross = forward(column(h, first), scale, lower)
            crossed = {(k, s): spread(cross[s][k : k + 1, :]) for s in range(W) for k in range(W)}
            corner = column(h, second)
            for t in range(W):
                for s in range(W):
                    corner[t] = corner[t] - cross[s] * crossed[t, s]
            scale2, lower2 = pivots(corner)
            others = range(h + 1, end)
            left = {i: column(i, first) for i in others}
            right = {i: column(i, second) for i in others}
            solved, group = solve_rows(rows[g], first, scale, lower)
            rows[g] = group
            solved2, group2 = solve_rows(take(rows[h], cross, solved, first), second, scale2, lower2)
            rows[h] = group2
            for i in others:
                one = forward(left[i], scale, lower)
                two = right[i]
                for t in range(W):
                    for s in range(W):
                        two[t] = two[t] - one[s] * crossed[t, s]
                two = forward(two, scale2, lower2)
                rows[i] = take(take(rows[i], one, solved, first), two, solved2, second)
        if end < n // W:
            edge = end * W
            kept = lambda g: jnp.where((lane < (g + 1) * W) | (lane >= edge), rows[g], 0.0)
            done = jnp.concatenate([kept(g) for g in range(p * per, end)], axis=0)
            pair = split(done)
            term = joined(pair, pair, (0, 0))
            outside = (lane < p * panel) | (lane >= (p + 1) * panel)
            for i in range(end, n // W):
                rows[i] = jnp.where(outside, rows[i], 0.0) - term[W * i : W * (i + 1), :]
    out = jnp.concatenate(rows, axis=0)
    down = lax.broadcasted_iota(jnp.int32, (n, n), 0)
    across = lax.broadcasted_iota(jnp.int32, (n, n), 1)
    return jnp.where(down >= across, out, 0.0)


def factor_kernel(diag_ref, high, low, work, beside=None):
    blocks, rows, order = diag_ref.shape
    work[...] = diag_ref[...]
    for i in range(blocks):
        for k in range(i, blocks):
            here = work[i, :, k * rows : (k + 1) * rows]
            there = work[k, :, i * rows : (i + 1) * rows]
            work[i, :, k * rows : (k + 1) * rows] = 0.5 * (here + there.T)
    down = lax.broadcasted_iota(jnp.int32, (rows, rows), 0)
    across = lax.broadcasted_iota(jnp.int32, (rows, rows), 1)
    unit = jnp.where(down == across, 1.0, 0.0)
    column_block = lax.broadcasted_iota(jnp.int32, (rows, order), 1) // rows

    def step(j, carry):
        at = pl.ds(pl.multiple_of(j * rows, rows), rows)
        if beside is not None:
            beside(j)
        inverse = factor_inverse(work[j, :, at])
        work[j, :, at] = unit
        solved = dot3(split(inverse), split(work[j]), 1)
        solved_high, solved_low = split(solved)
        high[at, :] = solved_high
        low[at, :] = solved_low
        for i in range(1, blocks):

            @pl.when(i > j)
            def _():
                cut = slice(i * rows, (i + 1) * rows)
                left = (high[at, cut], low[at, cut])
                work[i, :, at] = jnp.zeros((rows, rows), jnp.float32)
                work[i] = work[i] - dot3(left, (solved_high, solved_low), 0)

        keep = column_block <= j
        high[at, :] = jnp.where(keep, solved_high, 0.0).astype(jnp.bfloat16)
        low[at, :] = jnp.where(keep, solved_low, 0.0).astype(jnp.bfloat16)
        return carry

    lax.fori_loop(0, blocks, step, 0)


def put_terms(index, inverse_high, inverse_low, parts_ref, out_ref, high, low):
    blocks, _, rows, order = parts_ref.shape
    for part in range(2):
        across = slice(part * order, (part + 1) * order)
        right = [split(parts_ref[i, part]) for i in range(blocks)]
        right = [jnp.concatenate([r[k] for r in right], axis=0) for k in range(2)]
        for j in range(blocks):
            at, deep = slice(j * rows, (j + 1) * rows), (j + 1) * rows
            left = (inverse_high[at, :deep], inverse_low[at, :deep])
            solved = dot3(left, (right[0][:deep], right[1][:deep]), 1)
            solved_high, solved_low = split(solved)
            high[at, across] = solved_high
            low[at, across] = solved_low
    mine = index * rows
    for k, (first, second) in enumerate(((0, 0), (0, 1), (1, 1), (1, 0))):
        cut = pl.ds(pl.multiple_of(first * order + mine, rows), rows)
        across = slice(second * order, (second + 1) * order)
        out_ref[k] = dot3((high[:, cut], low[:, cut]), (high[:, across], low[:, across]), 0)


MESH = pl.DeviceIdType.MESH


def across(place, bit):
    return place + bit - 2 * bit * ((place // bit) % 2)


class Spread:
    def __init__(self, size, place, block, send_sem, recv_sem, own=None, cut=None, base=0):
        bits = [size >> (k + 1) for k in range(size.bit_length() - 1)]
        self.plan = [(b, 0) for b in bits]
        for k, b in enumerate(bits):
            earlier = [0]
            for e in bits[:k]:
                earlier += [m + e for m in earlier]
            self.plan += [(b, m) for m in earlier if m]
        self.copies, self.arrived = [], set()
        part = lambda held: block.at[held] if cut is None else block.at[held, cut]
        for k, (b, m) in enumerate(self.plan):
            held = place
            for e in bits:
                if m & e:
                    held = across(held, e)
            self.copies.append(
                pltpu.make_async_remote_copy(
                    src_ref=own if own is not None and m == 0 else part(held),
                    dst_ref=part(held),
                    send_sem=send_sem.at[base + k],
                    recv_sem=recv_sem.at[base + k],
                    device_id={"swath": across(place, b)},
                    device_id_type=MESH,
                )
            )

    def start_own(self):
        for copy, (b, m) in zip(self.copies, self.plan):
            if m == 0:
                copy.start()

    def forward(self):
        for copy, (b, m) in zip(self.copies, self.plan):
            if m:
                last = m & -m
                source = self.plan.index((last, m - last))
                if source not in self.arrived:
                    self.copies[source].wait_recv()
                    self.arrived.add(source)
                copy.start()

    def finish(self):
        for k, copy in enumerate(self.copies):
            if k not in self.arrived:
                copy.wait_recv()
        for copy in self.copies:
            copy.wait_send()


def greet(distance, times, size, spread_too):
    place, me = lax.axis_index("swath"), lax.axis_index("tm")
    barrier = pltpu.get_barrier_semaphore()
    behind, ahead = me >= distance, me + distance < times

    @pl.when(behind)
    def _():
        pl.semaphore_signal(barrier, inc=1, device_id={"tm": me - distance}, device_id_type=MESH)

    @pl.when(ahead)
    def _():
        pl.semaphore_signal(barrier, inc=1, device_id={"tm": me + distance}, device_id_type=MESH)

    count = behind.astype(jnp.int32) + ahead.astype(jnp.int32)
    if spread_too:
        bits = [size >> (k + 1) for k in range(size.bit_length() - 1)]
        for b in bits:
            pl.semaphore_signal(
                barrier, inc=1, device_id={"swath": across(place, b)}, device_id_type=MESH
            )
        count = count + len(bits)
    pl.semaphore_wait(barrier, count)
    return place, me, behind, ahead


def handed(me, distance, behind, ahead, moves, send_sem, recv_sem):
    plan = []
    for k, (source, target, up) in enumerate(moves):
        copy = pltpu.make_async_remote_copy(
            src_ref=source,
            dst_ref=target,
            send_sem=send_sem.at[k],
            recv_sem=recv_sem.at[k],
            device_id={"tm": me + distance if up else me - distance},
            device_id_type=MESH,
        )
        plan.append((copy, target, ahead if up else behind, behind if up else ahead))

    def start(items):
        for copy, target, sends, receives in items:
            pl.when(sends)(copy.start)

    def receive(items):
        for copy, target, sends, receives in items:
            pl.when(receives)(copy.wait_recv)

            @pl.when(jnp.logical_not(receives))
            def _():
                target[...] = jnp.zeros(target.shape, target.dtype)

    def sent(items):
        for copy, target, sends, receives in items:
            pl.when(sends)(copy.wait_send)

    return plan, start, receive, sent


def step_kernel(distance, times, size, terms_ref, diag_ref, out_ref, out_diag_ref, land, diag_full,
                parts, high, low, work, solved_high, solved_low, move_send, move_recv,
                diag_send, diag_recv, part_send, part_recv):
    place, me, behind, ahead = greet(distance, times, size, True)
    piece = diag_ref.shape[0] // PIECES
    cuts = [pl.ds(c * piece, piece) for c in range(PIECES)]
    moves = []
    for cut in cuts:
        moves.append((terms_ref.at[0, cut], land.at[0, cut], True))
        moves.append((terms_ref.at[2, cut], land.at[1, cut], False))
    moves.append((terms_ref.at[3], parts.at[place, 0], False))
    moves.append((terms_ref.at[1], parts.at[place, 1], True))
    plan, start, receive, sent = handed(
        me, distance, behind, ahead, moves, move_send, move_recv
    )
    coupled = 2 * PIECES
    start(plan[:coupled])
    spreads = []
    for c, cut in enumerate(cuts):
        receive(plan[2 * c : 2 * c + 2])
        if c == PIECES - 1:
            start(plan[coupled:])
        mine = diag_ref[cut] - land[0, cut] - land[1, cut]
        out_diag_ref[cut] = mine
        diag_full[place, cut] = mine
        spreads.append(
            Spread(size, place, diag_full, diag_send, diag_recv, None, cut, c * (size - 1))
        )
        spreads[c].start_own()
    for spread in spreads:
        spread.forward()
    for spread in spreads:
        spread.finish()
    part_spread = Spread(size, place, parts, part_send, part_recv)
    blocks = diag_full.shape[0]

    def beside(j):
        @pl.when(j == 1)
        def _():
            receive(plan[coupled:])
            part_spread.start_own()

        @pl.when(j == blocks - 1)
        def _():
            part_spread.forward()

    factor_kernel(diag_full, high, low, work, beside)
    part_spread.finish()
    sent(plan)
    put_terms(place, high, low, parts, out_ref, solved_high, solved_low)


def step(distance, terms_in, diag_rows):
    times, size = lax.axis_size("tm"), lax.axis_size("swath")
    rows, order = diag_rows.shape
    vmem = pl.BlockSpec(memory_space=pltpu.VMEM)
    dma = pltpu.SemaphoreType.DMA
    return pl.pallas_call(
        functools.partial(step_kernel, distance, times, size),
        out_shape=(
            jax.ShapeDtypeStruct((4, rows, order), jnp.float32),
            jax.ShapeDtypeStruct((rows, order), jnp.float32),
        ),
        in_specs=[vmem] * 2,
        out_specs=(vmem,) * 2,
        scratch_shapes=[
            pltpu.VMEM((2, rows, order), jnp.float32),
            pltpu.VMEM((size, rows, order), jnp.float32),
            pltpu.VMEM((size, 2, rows, order), jnp.float32),
            pltpu.VMEM((order, order), jnp.bfloat16),
            pltpu.VMEM((order, order), jnp.bfloat16),
            pltpu.VMEM((size, rows, order), jnp.float32),
            pltpu.VMEM((order, 2 * order), jnp.bfloat16),
            pltpu.VMEM((order, 2 * order), jnp.bfloat16),
            dma((2 * PIECES + 2,)),
            dma((2 * PIECES + 2,)),
            dma((PIECES * (size - 1),)),
            dma((PIECES * (size - 1),)),
            dma((size - 1,)),
            dma((size - 1,)),
        ],
        compiler_params=pltpu.CompilerParams(collective_id=distance, has_side_effects=True),
    )(terms_in, diag_rows)


def last_kernel(distance, times, size, terms_ref, diag_ref, out_diag_ref, out_coup_ref, land, move_send, move_recv):
    place, me, behind, ahead = greet(distance, times, size, False)
    moves = [
        (terms_ref.at[3], land.at[2], False),
        (terms_ref.at[0], land.at[0], True),
        (terms_ref.at[2], land.at[1], False),
    ]
    plan, start, receive, sent = handed(
        me, distance, behind, ahead, moves, move_send, move_recv
    )
    start(plan)
    receive(plan)
    out_coup_ref[...] = -land[2]
    out_diag_ref[...] = diag_ref[...] - land[0] - land[1]
    sent(plan)


def last(distance, terms_in, diag_rows):
    times, size = lax.axis_size("tm"), lax.axis_size("swath")
    rows, order = diag_rows.shape
    vmem = pl.BlockSpec(memory_space=pltpu.VMEM)
    return pl.pallas_call(
        functools.partial(last_kernel, distance, times, size),
        out_shape=(jax.ShapeDtypeStruct((rows, order), jnp.float32),) * 2,
        in_specs=[vmem] * 2,
        out_specs=(vmem,) * 2,
        scratch_shapes=[
            pltpu.VMEM((3, rows, order), jnp.float32),
            pltpu.SemaphoreType.DMA((3,)),
            pltpu.SemaphoreType.DMA((3,)),
        ],
        compiler_params=pltpu.CompilerParams(collective_id=distance, has_side_effects=True),
    )(terms_in, diag_rows)


def weigh_kernel(total_slots, block_rows, design_ref, process_ref, routes_ref, counts_ref, near_ref, sent_ref):
    me = lax.axis_index("tm")
    block_count = routes_ref.shape[1]
    slot_count = block_count // 2
    weighted = []
    for r in range(block_count):
        raw = design_ref[r * block_rows : (r + 1) * block_rows, :].astype(jnp.float32)
        mean_sq = jnp.mean(raw * raw, axis=-1, keepdims=True)
        weighted.append((raw * lax.rsqrt(4.0 * total_slots * (mean_sq + 1e-06))).astype(jnp.bfloat16))
    for out_ref, owner in ((near_ref, me), (sent_ref, me + 1)):
        place = jnp.int32(0)
        chosen = [jnp.full((), -1, jnp.int32) for _ in range(slot_count)]
        for r in range(block_count):
            named = routes_ref[0, r] == owner
            live = r < counts_ref[0, 0]
            for k in range(slot_count):
                chosen[k] = jnp.where(named & live & (place == k), r, chosen[k])
            place = place + named.astype(jnp.int32)
        for k in range(slot_count):
            block = jnp.zeros(weighted[0].shape, jnp.float32)
            for r in range(block_count):
                block = jnp.where(chosen[k] == r, weighted[r].astype(jnp.float32), block)
            out_ref[k * block_rows : (k + 1) * block_rows, :] = block.astype(jnp.bfloat16)
        out_ref[slot_count * block_rows :, :] = process_ref[...]


def weigh(design, process, routes, counts, total_slots):
    order = process.shape[1]
    block_count = routes.shape[1]
    block_rows = design.shape[0] // block_count
    rows = block_count // 2 * block_rows + process.shape[0]
    vmem, smem = (pl.BlockSpec(memory_space=m) for m in (pltpu.VMEM, pltpu.SMEM))
    return pl.pallas_call(
        functools.partial(weigh_kernel, total_slots, block_rows),
        out_shape=(jax.ShapeDtypeStruct((rows, order), jnp.bfloat16),) * 2,
        in_specs=[vmem, vmem, smem, smem],
        out_specs=(vmem,) * 2,
    )(design, process, routes, counts)


def first_kernel(times, size, near_ref, sent_ref, prior_ref, out_ref, out_diag_ref, near, far, prior,
                 diag_full, parts, high, low, work, solved_high, solved_low, move_send, move_recv,
                 near_send, near_recv, prior_send, prior_recv, far_send, far_recv):
    place, me, behind, ahead = greet(1, times, size, True)
    rows, order = diag_full.shape[1:]
    observed = near.shape[1] - rows
    piece = near.shape[1] // PIECES
    cuts = [pl.ds(c * piece, piece) for c in range(PIECES)]
    moves = [(sent_ref.at[cut], far.at[place, cut], True) for cut in cuts]
    plan, start, receive, sent = handed(me, 1, behind, ahead, moves, move_send, move_recv)
    start(plan)
    near_spread = Spread(size, place, near, near_send, near_recv, near_ref)
    prior_spread = Spread(size, place, prior, prior_send, prior_recv, prior_ref)
    near_spread.start_own()
    prior_spread.start_own()
    near[place] = near_ref[...]
    prior[place] = prior_ref[...]
    far_spreads = []
    for c, cut in enumerate(cuts):
        receive(plan[c : c + 1])
        far_spreads.append(
            Spread(size, place, far, far_send, far_recv, None, cut, c * (size - 1))
        )
        far_spreads[c].start_own()
    near_spread.forward()
    prior_spread.forward()
    near_spread.finish()
    prior_spread.finish()
    for spread in far_spreads:
        spread.forward()
    square = (rows, rows)
    unit = lax.broadcasted_iota(jnp.int32, square, 0) == lax.broadcasted_iota(jnp.int32, square, 1)

    def add_grams(source):
        for b in range(size):
            cut = slice(b * rows, (b + 1) * rows)
            total = source[b, observed:].astype(jnp.float32)
            for i in range(size):
                total = total + lax.dot_general(
                    source[i, :observed, cut],
                    source[i, :observed, :],
                    (((0,), (0,)), ((), ())),
                    preferred_element_type=jnp.float32,
                )
            yield b, cut, total

    for b, cut, total in add_grams(near):
        diag_full[b] = total
        diag_full[b, :, cut] += jnp.where(unit, jnp.broadcast_to(prior[b][:1], square), 0.0)
        parts[b, 0] = near[b, observed:].astype(jnp.float32)
    for spread in far_spreads:
        spread.finish()
    for b, cut, total in add_grams(far):
        diag_full[b] += total
        for q in range(size):
            turned = far[q, observed:, cut].astype(jnp.float32).T
            parts[b, 1, :, q * rows : (q + 1) * rows] = turned
    out_diag_ref[...] = diag_full[place]
    factor_kernel(diag_full, high, low, work)
    sent(plan)
    put_terms(place, high, low, parts, out_ref, solved_high, solved_low)


def first(near, sent, prior):
    times, size = lax.axis_size("tm"), lax.axis_size("swath")
    order = near.shape[1]
    rows = order // size
    vmem = pl.BlockSpec(memory_space=pltpu.VMEM)
    dma = pltpu.SemaphoreType.DMA
    return pl.pallas_call(
        functools.partial(first_kernel, times, size),
        out_shape=(
            jax.ShapeDtypeStruct((4, rows, order), jnp.float32),
            jax.ShapeDtypeStruct((rows, order), jnp.float32),
        ),
        in_specs=[vmem] * 3,
        out_specs=(vmem,) * 2,
        scratch_shapes=[
            pltpu.VMEM((size,) + near.shape, jnp.bfloat16),
            pltpu.VMEM((size,) + near.shape, jnp.bfloat16),
            pltpu.VMEM((size,) + prior.shape, jnp.float32),
            pltpu.VMEM((size, rows, order), jnp.float32),
            pltpu.VMEM((size, 2, rows, order), jnp.float32),
            pltpu.VMEM((order, order), jnp.bfloat16),
            pltpu.VMEM((order, order), jnp.bfloat16),
            pltpu.VMEM((size, rows, order), jnp.float32),
            pltpu.VMEM((order, 2 * order), jnp.bfloat16),
            pltpu.VMEM((order, 2 * order), jnp.bfloat16),
            dma((PIECES,)),
            dma((PIECES,)),
        ]
        + [dma((size - 1,))] * 4
        + [dma((PIECES * (size - 1),))] * 2,
        compiler_params=pltpu.CompilerParams(collective_id=0, has_side_effects=True),
    )(near, sent, prior)


def shards(design, process, prior_prec, routes, counts):
    row_count = process.shape[1]
    block_count = routes.shape[1]
    block_rows = design.shape[1] // block_count
    total_slots = 2 * (block_count // 2) * block_rows * lax.axis_size("swath")
    near, sent = weigh(design[0], process[0], routes, counts, total_slots)
    prior = jnp.broadcast_to(prior_prec, (8, row_count))
    out, diag_rows = first(near, sent, prior)
    for level in range(1, LEVELS):
        out, diag_rows = step(2 ** (level - 1), out, diag_rows)
    diag_rows, coup_rows = last(2 ** (LEVELS - 1), out, diag_rows)
    return (diag_rows[None], coup_rows[None])


def solution(mesh):
    return jax.shard_map(
        shards,
        mesh=mesh,
        in_specs=(
            P("tm", "swath", None),
            P("tm", "swath", None),
            P("tm", "swath"),
            P("tm", "swath"),
            P("tm", "swath"),
        ),
        out_specs=(P("tm", "swath", None), P("tm", "swath", None)),
        check_vma=False,
    )
```

```python
import functools

import jax
import jax.numpy as jnp
from jax import lax
from jax.experimental import pallas as pl
from jax.experimental.pallas import tpu as pltpu
from jax.sharding import PartitionSpec as P

LEVELS = 3
W = 8
MESH = pl.DeviceIdType.MESH


def split(x):
    high = x.astype(jnp.bfloat16)
    return high, (x - high.astype(jnp.float32)).astype(jnp.bfloat16)

def joined(a, b, dims):
    (ah, al), (bh, bl) = a, b
    return lax.dot_general(
        jnp.concatenate([ah, ah, al], axis=dims[0]),
        jnp.concatenate([bh, bl, bh], axis=dims[1]),
        (((dims[0],), (dims[1],)), ((), ())),
        preferred_element_type=jnp.float32,
    )

def pivots(columns):
    spread = lambda x: jnp.broadcast_to(x, columns[0].shape)
    entry = {(k, s): spread(columns[s][k : k + 1, :]) for s in range(W) for k in range(s, W)}
    scale, lower = [], {}
    for s in range(W):
        pivot = entry[s, s]
        turned = 1.0 / pivot
        scale.append(lax.rsqrt(pivot))
        if s + 1 < W:
            near = entry[s + 1, s]
            entry[s + 1, s + 1] = entry[s + 1, s + 1] - (near * near) * turned
        for k in range(s + 1, W):
            lower[k, s] = entry[k, s] * scale[s]
        for k in range(s + 2, W):
            part = entry[k, s] * turned
            for t in range(s + 1, k + 1):
                entry[k, t] = entry[k, t] - part * entry[t, s]
    return scale, lower

def forward(values, scale, lower):
    out = []
    values = list(values)
    for s in range(W):
        out.append(values[s] * scale[s])
        for k in range(s + 1, W):
            values[k] = values[k] - lower[k, s] * out[s]
    return out

def factor_inverse(m, panel=32):
    n = m.shape[0]
    rows = [m[W * g : W * (g + 1), :] for g in range(n // W)]
    lane = lax.broadcasted_iota(jnp.int32, (W, n), 1)
    sub = lax.broadcasted_iota(jnp.int32, (W, n), 0)
    spread = lambda x: jnp.broadcast_to(x, (W, n))
    cleared = lambda x, first: jnp.where((lane >= first) & (lane < first + W), 0.0, x)
    column = lambda h, first: [spread(rows[h][:, first + s : first + s + 1]) for s in range(W)]

    def solve_rows(row, first, scale, lower):
        row = cleared(row, first)
        start = [jnp.where(lane == first + s, 1.0, spread(row[s : s + 1, :])) for s in range(W)]
        solved = forward(start, scale, lower)
        group = solved[0]
        for s in range(1, W):
            group = jnp.where(sub == s, solved[s], group)
        return solved, group

    def take(row, factors, solved, first):
        row = cleared(row, first)
        for s in range(W):
            row = row - factors[s] * solved[s]
        return row

    per = panel // W
    for p in range(n // panel):
        end = (p + 1) * per
        for q in range(0, per, 2):
            g, h = p * per + q, p * per + q + 1
            first, second = g * W, h * W
            scale, lower = pivots(column(g, first))
            cross = forward(column(h, first), scale, lower)
            crossed = {(k, s): spread(cross[s][k : k + 1, :]) for s in range(W) for k in range(W)}
            corner = column(h, second)
            for t in range(W):
                for s in range(W):
                    corner[t] = corner[t] - cross[s] * crossed[t, s]
            scale2, lower2 = pivots(corner)
            others = range(h + 1, end)
            left = {i: column(i, first) for i in others}
            right = {i: column(i, second) for i in others}
            solved, group = solve_rows(rows[g], first, scale, lower)
            rows[g] = group
            solved2, group2 = solve_rows(take(rows[h], cross, solved, first), second, scale2, lower2)
            rows[h] = group2
            for i in others:
                one = forward(left[i], scale, lower)
                two = right[i]
                for t in range(W):
                    for s in range(W):
                        two[t] = two[t] - one[s] * crossed[t, s]
                two = forward(two, scale2, lower2)
                rows[i] = take(take(rows[i], one, solved, first), two, solved2, second)
        if end < n // W:
            edge = end * W
            kept = lambda g: jnp.where((lane < (g + 1) * W) | (lane >= edge), rows[g], 0.0)
            done = jnp.concatenate([kept(g) for g in range(p * per, end)], axis=0)
            pair = split(done)
            term = joined(pair, pair, (0, 0))
            outside = (lane < p * panel) | (lane >= (p + 1) * panel)
            for i in range(end, n // W):
                rows[i] = jnp.where(outside, rows[i], 0.0) - term[W * i : W * (i + 1), :]
    out = jnp.concatenate(rows, axis=0)
    down = lax.broadcasted_iota(jnp.int32, (n, n), 0)
    across = lax.broadcasted_iota(jnp.int32, (n, n), 1)
    return jnp.where(down >= across, out, 0.0)


def plain(a, b):
    return lax.dot_general(a, b, (((1,), (0,)), ((), ())), preferred_element_type=jnp.float32)


def factor(work, high, low, beside=None):
    blocks, rows, order = work.shape
    down = lax.broadcasted_iota(jnp.int32, (rows, rows), 0)
    across = lax.broadcasted_iota(jnp.int32, (rows, rows), 1)
    unit = jnp.where(down == across, 1.0, 0.0)
    column_block = lax.broadcasted_iota(jnp.int32, (rows, order), 1) // rows

    def step(j, carry):
        at = pl.ds(pl.multiple_of(j * rows, rows), rows)
        if beside is not None:
            beside(j)
        inverse = factor_inverse(work[j, :, at])
        work[j, :, at] = unit
        solved = joined(split(inverse), split(work[j]), (1, 0))
        solved_high, solved_low = split(solved)
        high[at, :] = solved_high
        low[at, :] = solved_low
        for i in range(1, blocks):

            @pl.when(i > j)
            def _():
                cut = slice(i * rows, (i + 1) * rows)
                left = (high[at, cut].T, low[at, cut].T)
                work[i, :, at] = jnp.zeros((rows, rows), jnp.float32)
                work[i] = work[i] - joined(left, (solved_high, solved_low), (1, 0))

        keep = column_block <= j
        high[at, :] = jnp.where(keep, solved_high, 0.0).astype(jnp.bfloat16)
        low[at, :] = jnp.where(keep, solved_low, 0.0).astype(jnp.bfloat16)
        return carry

    lax.fori_loop(0, blocks, step, 0)


def solve(high, low, right_high, right_low, out_high, out_low, part, blocks):
    order = high.shape[0]
    rows = order // blocks
    across = slice(part * order, (part + 1) * order)
    for j in range(blocks):
        at, deep = slice(j * rows, (j + 1) * rows), (j + 1) * rows
        left = (high[at, :deep], low[at, :deep])
        top = right_high[:deep, across]
        if right_low is None:
            solved = plain(left[0], top) + plain(left[1], top)
        else:
            solved = joined(left, (top, right_low[:deep, across]), (1, 0))
        solved_high, solved_low = split(solved)
        out_high[at, across] = solved_high
        out_low[at, across] = solved_low


def flipped(place, bit):
    return place + bit - 2 * bit * ((place // bit) % 2)


class Spread:
    def __init__(self, size, place, view, send_sem, recv_sem, base=0, own=None):
        bits = [size >> (k + 1) for k in range(size.bit_length() - 1)]
        self.plan = [(b, 0) for b in bits]
        for k, b in enumerate(bits):
            earlier = [0]
            for e in bits[:k]:
                earlier += [m + e for m in earlier]
            self.plan += [(b, m) for m in earlier if m]
        self.source = {}
        for b, m in self.plan:
            if m:
                last = m & -m
                self.source[b, m] = self.plan.index((last, m - last))
        self.copies = []
        for k, (b, m) in enumerate(self.plan):
            held = place
            for e in bits:
                if m & e:
                    held = flipped(held, e)
            self.copies.append(
                pltpu.make_async_remote_copy(
                    src_ref=own if own is not None and m == 0 else view(held),
                    dst_ref=view(held),
                    send_sem=send_sem.at[base + k],
                    recv_sem=recv_sem.at[base + k],
                    device_id={"swath": flipped(place, b)},
                    device_id_type=MESH,
                )
            )

    def start_own(self):
        for copy, (b, m) in zip(self.copies, self.plan):
            if m == 0:
                copy.start()

    def forward(self):
        waited = set()
        for copy, item in zip(self.copies, self.plan):
            if item in self.source:
                source = self.source[item]
                if source not in waited:
                    self.copies[source].wait_recv()
                    waited.add(source)
                copy.start()

    def finish(self):
        waited = set(self.source.values())
        for k, copy in enumerate(self.copies):
            if k not in waited:
                copy.wait_recv()

    def sent(self):
        for copy in self.copies:
            copy.wait_send()


class Move:
    def __init__(self, source, target, send_sem, recv_sem, index, device, sends, receives):
        self.copy = pltpu.make_async_remote_copy(
            src_ref=source,
            dst_ref=target,
            send_sem=send_sem.at[index],
            recv_sem=recv_sem.at[index],
            device_id={"tm": device},
            device_id_type=MESH,
        )
        self.target, self.sends, self.receives = target, sends, receives

    def start(self):
        pl.when(self.sends)(self.copy.start)

    def receive(self):
        pl.when(self.receives)(self.copy.wait_recv)

        @pl.when(jnp.logical_not(self.receives))
        def _():
            self.target[...] = jnp.zeros(self.target.shape, self.target.dtype)

    def sent(self):
        pl.when(self.sends)(self.copy.wait_send)


def greet(times, size, place, me):
    barrier = pltpu.get_barrier_semaphore()
    count = jnp.int32(size - 1)
    for level in range(LEVELS):
        distance = 2**level
        for there, other in ((me >= distance, me - distance), (me + distance < times, me + distance)):

            @pl.when(there)
            def _():
                pl.semaphore_signal(barrier, inc=1, device_id={"tm": other}, device_id_type=MESH)

            count = count + there.astype(jnp.int32)
    for d in range(1, size):
        pl.semaphore_signal(
            barrier, inc=1, device_id={"swath": (place + d) % size}, device_id_type=MESH
        )
    return barrier, count


def pick(weighted, routes_ref, counts_ref, owner, slot):
    block_count = routes_ref.shape[1]
    place = jnp.int32(0)
    chosen = jnp.full((), -1, jnp.int32)
    for r in range(block_count):
        named = routes_ref[0, r] == owner
        live = r < counts_ref[0, 0]
        chosen = jnp.where(named & live & (place == slot), r, chosen)
        place = place + named.astype(jnp.int32)
    block = jnp.zeros(weighted[0].shape, jnp.float32)
    for r in range(block_count):
        block = jnp.where(chosen == r, weighted[r], block)
    return block.astype(jnp.bfloat16)


def kernel(times, size, total_slots, block_rows, design_ref, process_ref, prior_ref, routes_ref,
           counts_ref, out_diag_ref, out_coup_ref, obs, proc, leaving, prior, skew, work, high, low,
           right_high, right_low, solved_high, solved_low, parts, shares, land, terms, cross, corner,
           last_cross, last_full, last_half, first_send, first_recv, spread_send, spread_recv,
           prior_send, prior_recv, term_send, term_recv, cross_send, cross_recv, share_send,
           share_recv, part_send, part_recv, last_send, last_recv):
    place, me = lax.axis_index("swath"), lax.axis_index("tm")
    rows, order = process_ref.shape
    block_count = routes_ref.shape[1]
    slot_count = block_count // 2
    reach, half = size // 2, rows // 2
    hops = size - 1
    barrier, count = greet(times, size, place, me)

    weighted = []
    for r in range(block_count):
        raw = design_ref[r * block_rows : (r + 1) * block_rows, :].astype(jnp.float32)
        mean_sq = jnp.mean(raw * raw, axis=-1, keepdims=True)
        weighted.append(raw * lax.rsqrt(4.0 * total_slots * (mean_sq + 1e-06)))
    for slot in range(slot_count):
        cut = slice(slot * block_rows, (slot + 1) * block_rows)
        leaving[cut, :] = pick(weighted, routes_ref, counts_ref, me + 1, slot)
        obs[0, place, cut, :] = pick(weighted, routes_ref, counts_ref, me, slot)
    pl.semaphore_wait(barrier, count)

    behind, ahead = me >= 1, me + 1 < times
    spread = lambda view, k, own=None: Spread(
        size, place, view, spread_send, spread_recv, k * hops, own
    )
    slots = [pl.ds(c * block_rows, block_rows) for c in range(slot_count)]
    far_moves = [
        Move(process_ref, proc.at[1, place], first_send, first_recv, 0, me + 1, ahead, behind)
    ]
    for c, cut in enumerate(slots):
        far_moves.append(
            Move(leaving.at[cut], obs.at[1, place, cut], first_send, first_recv, c + 1, me + 1,
                 ahead, behind)
        )
    for move in far_moves:
        move.start()
    near_proc = spread(lambda held: proc.at[0, held], 0, process_ref)
    near_prior = Spread(size, place, lambda held: prior.at[held], prior_send, prior_recv, 0, prior_ref)
    near_obs = spread(lambda held: obs.at[0, held], 1)
    near_proc.start_own()
    near_prior.start_own()
    near_obs.start_own()
    proc[0, place] = process_ref[...]
    prior[place] = prior_ref[...]
    far_proc = spread(lambda held: proc.at[1, held], 2)
    far_obs = [
        spread(lambda held, cut=cut: obs.at[1, held, cut], 3 + c) for c, cut in enumerate(slots)
    ]
    far_moves[0].receive()
    far_proc.start_own()
    near_proc.forward()
    near_prior.forward()
    for c in range(slot_count):
        far_moves[c + 1].receive()
        far_obs[c].start_own()
    near_obs.forward()
    far_proc.forward()
    near_proc.finish()
    near_prior.finish()
    near_obs.finish()

    def gram(which, cut, b):
        total = None
        for i in range(size):
            term = lax.dot_general(
                obs[which, i, cut, b * rows : (b + 1) * rows],
                obs[which, i, cut, b * rows :],
                (((0,), (0,)), ((), ())),
                preferred_element_type=jnp.float32,
            )
            total = term if total is None else total + term
        return total

    square = (rows, rows)
    unit = lax.broadcasted_iota(jnp.int32, square, 0) == lax.broadcasted_iota(jnp.int32, square, 1)
    cuts = [slice(b * rows, (b + 1) * rows) for b in range(size)]
    for b in range(size):
        work[b, :, b * rows :] = gram(0, slice(None), b)
        work[b, :, cuts[b]] += jnp.where(unit, jnp.broadcast_to(prior[b][:1], square), 0.0)
        right_high[cuts[b], :order] = proc[0, b]
    far_proc.finish()
    both = lambda a, b: proc[0, a, :, cuts[b]].astype(jnp.float32) + proc[1, a, :, cuts[b]].astype(
        jnp.float32
    )
    for b in range(size):
        for q in range(size):
            right_high[cuts[b], order + q * rows : order + (q + 1) * rows] = proc[1, q, :, cuts[b]].T
            if q >= b:
                work[b, :, cuts[q]] += 0.5 * (both(b, q) + both(q, b).T)
    for c in range(slot_count):
        far_obs[c].forward()
        far_obs[c].finish()
        for b in range(size):
            work[b, :, b * rows :] += gram(1, slots[c], b)
    for s in range(size):

        @pl.when(place == s)
        def _():
            for d in range(reach):
                q = (s + d) % size
                block = work[s, :, cuts[q]] if q >= s else work[q, :, cuts[s]].T
                shares[0, s, d * rows : (d + 1) * rows] = block
            a, h = s % reach, s // reach
            shares[0, s, reach * rows :] = work[a, h * half : (h + 1) * half, cuts[a + reach]]

    piece = rows // size
    sending = []
    column = lambda part, b: pl.ds(pl.multiple_of(part * order + b * rows, rows), rows)
    share_cuts = [pl.ds(d * rows, rows) for d in range(reach)] + [pl.ds(reach * rows, half)]
    for level in range(LEVELS):
        distance = 2**level
        last = level == LEVELS - 1
        behind, ahead = me >= distance, me + distance < times
        if level == 0:
            factor(work, high, low)
        else:
            arrivals = parts.at[level - 1]
            below = 2 ** (level - 1)
            has_next = me + 2 * below <= times
            has_previous = me >= 2 * below

            def part_spread(c, arrivals=arrivals, level=level):
                cut = pl.ds(pl.multiple_of(c * piece, piece), piece)
                return Spread(
                    size, place, lambda held: arrivals.at[held, :, cut], part_send, part_recv,
                    ((level - 1) * size + c) * hops,
                )

            def beside(j, arrivals=arrivals, level=level, below=below, has_next=has_next,
                       has_previous=has_previous, part_spread=part_spread):
                cut = pl.ds(pl.multiple_of(j * piece, piece), piece)
                index = ((level - 1) * size + j) * 2
                Move(cross.at[level - 1, 0, cut], arrivals.at[place, 0, cut], cross_send, cross_recv,
                     index, me, has_next, has_next).receive()
                Move(cross.at[level - 1, 1, cut], arrivals.at[place, 1, cut], cross_send, cross_recv,
                     index + 1, me, has_previous, has_previous).receive()
                part_spread(j).start_own()

                @pl.when(j > 0)
                def _():
                    part_spread(j - 1).forward()

            factor(work, high, low, beside)
            part_spread(size - 1).forward()
            for c in range(size):
                part_spread(c).finish()
                sending.append(part_spread(c))
            for b in range(size):
                for part in range(2):
                    top, bottom = split(arrivals[b, part])
                    right_high[cuts[b], part * order : (part + 1) * order] = top
                    right_low[cuts[b], part * order : (part + 1) * order] = bottom

        lower = None if level == 0 else right_low
        term_moves, turned = [], []
        for part in range(2):
            solve(high, low, right_high, lower, solved_high, solved_low, part, size)
            pair = lambda b, part=part: (solved_high[:, column(part, b)], solved_low[:, column(part, b)])
            own = pair(place)
            own = (own[0].T, own[1].T)
            turned.append(own)
            wide = [pair((place + d) % size) for d in range(reach)]
            wide = tuple(jnp.concatenate([w[k] for w in wide], axis=1) for k in range(2))
            product = joined(own, wide, (1, 0))
            for d in range(reach):
                terms[level, part, d * rows : (d + 1) * rows] = product[:, d * rows : (d + 1) * rows]
            a, h = place % reach, place // reach
            first = pair(a)
            corner[...] = joined((first[0].T, first[1].T), pair(a + reach), (1, 0))
            terms[level, part, reach * rows :] = corner[pl.ds(pl.multiple_of(h * half, half), half), :]
            sends, receives = (ahead, behind) if part == 0 else (behind, ahead)
            for d, cut in enumerate(share_cuts):
                move = Move(
                    terms.at[level, part, cut], land.at[level, part, cut], term_send, term_recv,
                    (level * 2 + part) * len(share_cuts) + d,
                    me + distance if part == 0 else me - distance, sends, receives,
                )
                move.start()
                term_moves.append(move)

        cross_moves = []
        goes_down = behind & (me + distance <= times)
        comes_down = me + 2 * distance <= times
        whole = lambda part: (
            solved_high[:, part * order : (part + 1) * order],
            solved_low[:, part * order : (part + 1) * order],
        )
        cross[level, 0] = joined(turned[1], whole(0), (1, 0))
        if last:
            final = Move(
                cross.at[level, 0], last_cross, last_send, last_recv, 0, me - distance, goes_down,
                comes_down,
            )
            final.start()
        else:
            cross[level, 1] = joined(turned[0], whole(1), (1, 0))
            target = parts.at[level]
            for c in range(size):
                cut = pl.ds(c * piece, piece)
                index = (level * size + c) * 2
                cross_moves.append(
                    Move(cross.at[level, 0, cut], target.at[place, 0, cut], cross_send, cross_recv,
                         index, me - distance, goes_down, comes_down)
                )
                cross_moves.append(
                    Move(cross.at[level, 1, cut], target.at[place, 1, cut], cross_send, cross_recv,
                         index + 1, me + distance, behind & ahead, me >= 2 * distance)
                )
            for move in cross_moves:
                move.start()

        spreads = []
        for d, cut in enumerate(share_cuts):
            term_moves[d].receive()
            term_moves[len(share_cuts) + d].receive()
            shares[level + 1, place, cut] = (
                shares[level, place, cut] - land[level, 0, cut] - land[level, 1, cut]
            )
            if not last:
                spreads.append(
                    Spread(size, place, lambda held, cut=cut: shares.at[level + 1, held, cut],
                           share_send, share_recv, (level * len(share_cuts) + d) * hops)
                )
                spreads[-1].start_own()
        sending += term_moves + cross_moves + spreads
        if level == 0:
            mine = pl.ds(pl.multiple_of(place * rows, rows), rows)
            for q in range(size):
                there = proc[0, q, :, mine].astype(jnp.float32) + proc[1, q, :, mine].astype(jnp.float32)
                here = proc[0, place, :, cuts[q]].astype(jnp.float32) + proc[
                    1, place, :, cuts[q]
                ].astype(jnp.float32)
                skew[:, cuts[q]] = 0.5 * (here - there.T)
        if not last:
            for one in spreads:
                one.forward()
            for one in spreads:
                one.finish()
            held = shares.at[level + 1]
            for s in range(size):
                for d in range(reach):
                    q = (s + d) % size
                    block = held[s, d * rows : (d + 1) * rows]
                    if q >= s:
                        work[s, :, cuts[q]] = block
                    else:
                        work[q, :, cuts[s]] = block.T
                a, h = s % reach, s // reach
                work[a, h * half : (h + 1) * half, cuts[a + reach]] = held[s, reach * rows :]

    copies = []
    for d in range(1, reach):
        copies.append(
            pltpu.make_async_remote_copy(
                src_ref=shares.at[LEVELS, place, share_cuts[d]],
                dst_ref=last_full.at[d - 1],
                send_sem=last_send.at[d],
                recv_sem=last_recv.at[d],
                device_id={"swath": (place + d) % size},
                device_id_type=MESH,
            )
        )
    copies.append(
        pltpu.make_async_remote_copy(
            src_ref=shares.at[LEVELS, place, share_cuts[reach]],
            dst_ref=last_half,
            send_sem=last_send.at[reach],
            recv_sem=last_recv.at[reach],
            device_id={"swath": (place + reach) % size},
            device_id_type=MESH,
        )
    )
    for copy in copies:
        copy.start()
    final.receive()
    out_coup_ref[...] = -last_cross[...]
    for copy in copies:
        copy.wait_recv()
    for s in range(size):

        @pl.when(place == s)
        def _():
            own = shares.at[LEVELS, s]
            for d in range(reach):
                q = (s + d) % size
                out_diag_ref[:, cuts[q]] = own[d * rows : (d + 1) * rows] + skew[:, cuts[q]]
            for d in range(1, reach):
                q = (s - d) % size
                out_diag_ref[:, cuts[q]] = last_full[d - 1].T + skew[:, cuts[q]]
            pieces = [own[reach * rows :], last_half[...]]
            if s < reach:
                block = jnp.concatenate(pieces, axis=0)
            else:
                block = jnp.concatenate(pieces[::-1], axis=0).T
            q = (s + reach) % size
            out_diag_ref[:, cuts[q]] = block + skew[:, cuts[q]]

    for copy in copies:
        copy.wait_send()
    final.sent()
    for move in far_moves + sending:
        move.sent()
    for one in [near_proc, near_prior, near_obs, far_proc] + far_obs:
        one.sent()


def shards(design, process, prior_prec, routes, counts):
    times, size = lax.axis_size("tm"), lax.axis_size("swath")
    rows, order = process.shape[1:]
    block_count = routes.shape[1]
    block_rows = design.shape[1] // block_count
    slot_count = block_count // 2
    observed = slot_count * block_rows
    total_slots = 2 * observed * size
    share = rows * (size // 2) + rows // 2
    hops = size - 1
    kinds = size // 2 + 1
    prior = jnp.broadcast_to(prior_prec, (8, rows))
    vmem, smem = (pl.BlockSpec(memory_space=m) for m in (pltpu.VMEM, pltpu.SMEM))
    f32, bf16 = jnp.float32, jnp.bfloat16
    dma = lambda n: [pltpu.SemaphoreType.DMA((n,))] * 2
    diag_rows, coup_rows = pl.pallas_call(
        functools.partial(kernel, times, size, total_slots, block_rows),
        out_shape=(jax.ShapeDtypeStruct((rows, order), f32),) * 2,
        in_specs=[vmem, vmem, vmem, smem, smem],
        out_specs=(vmem,) * 2,
        scratch_shapes=[
            pltpu.VMEM((2, size, observed, order), bf16),
            pltpu.VMEM((2, size, rows, order), bf16),
            pltpu.VMEM((observed, order), bf16),
            pltpu.VMEM((size,) + prior.shape, f32),
            pltpu.VMEM((rows, order), f32),
            pltpu.VMEM((size, rows, order), f32),
            pltpu.VMEM((order, order), bf16),
            pltpu.VMEM((order, order), bf16),
            pltpu.VMEM((order, 2 * order), bf16),
            pltpu.VMEM((order, 2 * order), bf16),
            pltpu.VMEM((order, 2 * order), bf16),
            pltpu.VMEM((order, 2 * order), bf16),
            pltpu.VMEM((LEVELS - 1, size, 2, rows, order), f32),
            pltpu.VMEM((LEVELS + 1, size, share, rows), f32),
            pltpu.VMEM((LEVELS, 2, share, rows), f32),
            pltpu.VMEM((LEVELS, 2, share, rows), f32),
            pltpu.VMEM((LEVELS, 2, rows, order), f32),
            pltpu.VMEM((rows, rows), f32),
            pltpu.VMEM((rows, order), f32),
            pltpu.VMEM((max(size // 2 - 1, 1), rows, rows), f32),
            pltpu.VMEM((rows // 2, rows), f32),
        ]
        + dma(1 + slot_count)
        + dma((3 + slot_count) * hops)
        + dma(hops)
        + dma(LEVELS * 2 * kinds)
        + dma((LEVELS - 1) * size * 2)
        + dma((LEVELS - 1) * kinds * hops)
        + dma((LEVELS - 1) * size * hops)
        + dma(kinds),
        compiler_params=pltpu.CompilerParams(collective_id=0, has_side_effects=True),
    )(design[0], process[0], prior, routes, counts)
    return (diag_rows[None], coup_rows[None])


def solution(mesh):
    return jax.shard_map(
        shards,
        mesh=mesh,
        in_specs=(
            P("tm", "swath", None),
            P("tm", "swath", None),
            P("tm", "swath"),
            P("tm", "swath"),
            P("tm", "swath"),
        ),
        out_specs=(P("tm", "swath", None), P("tm", "swath", None)),
        check_vma=False,
    )
```

```python
import functools

import jax
import jax.numpy as jnp
from jax import lax
from jax.experimental import pallas as pl
from jax.experimental.pallas import tpu as pltpu
from jax.sharding import PartitionSpec as P

LEVELS = 3
W = 8
PLAN = (((0, 3), (2, 5), (4, 7), (5, 8)), ((0, 3), (1, 5), (2, 6), (3, 7)))
MESH = pl.DeviceIdType.MESH


def split(x):
    high = x.astype(jnp.bfloat16)
    return high, (x - high.astype(jnp.float32)).astype(jnp.bfloat16)

def joined(a, b, dims):
    (ah, al), (bh, bl) = a, b
    return lax.dot_general(
        jnp.concatenate([ah, ah, al], axis=dims[0]),
        jnp.concatenate([bh, bl, bh], axis=dims[1]),
        (((dims[0],), (dims[1],)), ((), ())),
        preferred_element_type=jnp.float32,
    )

def pivots(columns):
    spread = lambda x: jnp.broadcast_to(x, columns[0].shape)
    entry = {(k, s): spread(columns[s][k : k + 1, :]) for s in range(W) for k in range(s, W)}
    scale, lower = [], {}
    for s in range(W):
        pivot = entry[s, s]
        turned = 1.0 / pivot
        scale.append(lax.rsqrt(pivot))
        if s + 1 < W:
            near = entry[s + 1, s]
            entry[s + 1, s + 1] = entry[s + 1, s + 1] - (near * near) * turned
        for k in range(s + 1, W):
            lower[k, s] = entry[k, s] * scale[s]
        for k in range(s + 2, W):
            part = entry[k, s] * turned
            for t in range(s + 1, k + 1):
                entry[k, t] = entry[k, t] - part * entry[t, s]
    return scale, lower

def forward(values, scale, lower):
    out = []
    values = list(values)
    for s in range(W):
        out.append(values[s] * scale[s])
        for k in range(s + 1, W):
            values[k] = values[k] - lower[k, s] * out[s]
    return out

def factor_inverse(m, panel=32):
    n = m.shape[0]
    rows = [m[W * g : W * (g + 1), :] for g in range(n // W)]
    lane = lax.broadcasted_iota(jnp.int32, (W, n), 1)
    sub = lax.broadcasted_iota(jnp.int32, (W, n), 0)
    spread = lambda x: jnp.broadcast_to(x, (W, n))
    cleared = lambda x, first: jnp.where((lane >= first) & (lane < first + W), 0.0, x)
    column = lambda h, first: [spread(rows[h][:, first + s : first + s + 1]) for s in range(W)]

    def solve_rows(row, first, scale, lower):
        row = cleared(row, first)
        start = [jnp.where(lane == first + s, 1.0, spread(row[s : s + 1, :])) for s in range(W)]
        solved = forward(start, scale, lower)
        group = solved[0]
        for s in range(1, W):
            group = jnp.where(sub == s, solved[s], group)
        return solved, group

    def take(row, factors, solved, first):
        row = cleared(row, first)
        for s in range(W):
            row = row - factors[s] * solved[s]
        return row

    per = panel // W
    for p in range(n // panel):
        end = (p + 1) * per
        for q in range(0, per, 2):
            g, h = p * per + q, p * per + q + 1
            first, second = g * W, h * W
            scale, lower = pivots(column(g, first))
            cross = forward(column(h, first), scale, lower)
            crossed = {(k, s): spread(cross[s][k : k + 1, :]) for s in range(W) for k in range(W)}
            corner = column(h, second)
            for t in range(W):
                for s in range(W):
                    corner[t] = corner[t] - cross[s] * crossed[t, s]
            scale2, lower2 = pivots(corner)
            others = range(h + 1, end)
            left = {i: column(i, first) for i in others}
            right = {i: column(i, second) for i in others}
            solved, group = solve_rows(rows[g], first, scale, lower)
            rows[g] = group
            solved2, group2 = solve_rows(take(rows[h], cross, solved, first), second, scale2, lower2)
            rows[h] = group2
            for i in others:
                one = forward(left[i], scale, lower)
                two = right[i]
                for t in range(W):
                    for s in range(W):
                        two[t] = two[t] - one[s] * crossed[t, s]
                two = forward(two, scale2, lower2)
                rows[i] = take(take(rows[i], one, solved, first), two, solved2, second)
        if end < n // W:
            edge = end * W
            kept = lambda g: jnp.where((lane < (g + 1) * W) | (lane >= edge), rows[g], 0.0)
            done = jnp.concatenate([kept(g) for g in range(p * per, end)], axis=0)
            pair = split(done)
            term = joined(pair, pair, (0, 0))
            outside = (lane < p * panel) | (lane >= (p + 1) * panel)
            for i in range(end, n // W):
                rows[i] = jnp.where(outside, rows[i], 0.0) - term[W * i : W * (i + 1), :]
    out = jnp.concatenate(rows, axis=0)
    down = lax.broadcasted_iota(jnp.int32, (n, n), 0)
    across = lax.broadcasted_iota(jnp.int32, (n, n), 1)
    return jnp.where(down >= across, out, 0.0)


def plain(a, b):
    return lax.dot_general(a, b, (((1,), (0,)), ((), ())), preferred_element_type=jnp.float32)


def factor(work, high, low, beside=None):
    blocks, rows, order = work.shape
    down = lax.broadcasted_iota(jnp.int32, (rows, rows), 0)
    across = lax.broadcasted_iota(jnp.int32, (rows, rows), 1)
    unit = jnp.where(down == across, 1.0, 0.0)
    column_block = lax.broadcasted_iota(jnp.int32, (rows, order), 1) // rows

    def step(j, carry):
        at = pl.ds(pl.multiple_of(j * rows, rows), rows)
        if beside is not None:
            beside(j, 0)
        inverse = factor_inverse(work[j, :, at])
        if beside is not None:
            beside(j, 1)
        work[j, :, at] = unit
        solved = joined(split(inverse), split(work[j]), (1, 0))
        solved_high, solved_low = split(solved)
        high[at, :] = solved_high
        low[at, :] = solved_low
        for i in range(1, blocks):

            @pl.when(i > j)
            def _():
                cut = slice(i * rows, (i + 1) * rows)
                left = (high[at, cut].T, low[at, cut].T)
                work[i, :, at] = jnp.zeros((rows, rows), jnp.float32)
                work[i] = work[i] - joined(left, (solved_high, solved_low), (1, 0))

        keep = column_block <= j
        high[at, :] = jnp.where(keep, solved_high, 0.0).astype(jnp.bfloat16)
        low[at, :] = jnp.where(keep, solved_low, 0.0).astype(jnp.bfloat16)
        return carry

    lax.fori_loop(0, blocks, step, 0)


def solve(high, low, right_high, right_low, out_high, out_low, part, blocks):
    order = high.shape[0]
    rows = order // blocks
    across = slice(part * order, (part + 1) * order)
    for j in range(blocks):
        at, deep = slice(j * rows, (j + 1) * rows), (j + 1) * rows
        left = (high[at, :deep], low[at, :deep])
        top = right_high[:deep, across]
        if right_low is None:
            solved = plain(left[0], top) + plain(left[1], top)
        else:
            solved = joined(left, (top, right_low[:deep, across]), (1, 0))
        solved_high, solved_low = split(solved)
        out_high[at, across] = solved_high
        out_low[at, across] = solved_low


def flipped(place, bit):
    return place + bit - 2 * bit * ((place // bit) % 2)


class Spread:
    def __init__(self, size, place, view, send_sem, recv_sem, base=0, own=None):
        bits = [size >> (k + 1) for k in range(size.bit_length() - 1)]
        self.plan = [(b, 0) for b in bits]
        for k, b in enumerate(bits):
            earlier = [0]
            for e in bits[:k]:
                earlier += [m + e for m in earlier]
            self.plan += [(b, m) for m in earlier if m]
        self.source = {}
        for b, m in self.plan:
            if m:
                last = m & -m
                self.source[b, m] = self.plan.index((last, m - last))
        self.copies = []
        for k, (b, m) in enumerate(self.plan):
            held = place
            for e in bits:
                if m & e:
                    held = flipped(held, e)
            self.copies.append(
                pltpu.make_async_remote_copy(
                    src_ref=own if own is not None and m == 0 else view(held),
                    dst_ref=view(held),
                    send_sem=send_sem.at[base + k],
                    recv_sem=recv_sem.at[base + k],
                    device_id={"swath": flipped(place, b)},
                    device_id_type=MESH,
                )
            )

    def start_own(self):
        for copy, (b, m) in zip(self.copies, self.plan):
            if m == 0:
                copy.start()

    def forward(self):
        waited = set()
        for copy, item in zip(self.copies, self.plan):
            if item in self.source:
                source = self.source[item]
                if source not in waited:
                    self.copies[source].wait_recv()
                    waited.add(source)
                copy.start()

    def finish(self):
        waited = set(self.source.values())
        for k, copy in enumerate(self.copies):
            if k not in waited:
                copy.wait_recv()

    def sent(self):
        for copy in self.copies:
            copy.wait_send()


class Move:
    def __init__(self, source, target, send_sem, recv_sem, index, device, sends, receives):
        self.copy = pltpu.make_async_remote_copy(
            src_ref=source,
            dst_ref=target,
            send_sem=send_sem.at[index],
            recv_sem=recv_sem.at[index],
            device_id={"tm": device},
            device_id_type=MESH,
        )
        self.target, self.sends, self.receives = target, sends, receives

    def start(self):
        pl.when(self.sends)(self.copy.start)

    def receive(self):
        pl.when(self.receives)(self.copy.wait_recv)

        @pl.when(jnp.logical_not(self.receives))
        def _():
            self.target[...] = jnp.zeros(self.target.shape, self.target.dtype)

    def sent(self):
        pl.when(self.sends)(self.copy.wait_send)


def greet(times, size, place, me):
    barrier = pltpu.get_barrier_semaphore()
    count = jnp.int32(size - 1)
    for level in range(LEVELS):
        distance = 2**level
        for there, other in ((me >= distance, me - distance), (me + distance < times, me + distance)):

            @pl.when(there)
            def _():
                pl.semaphore_signal(barrier, inc=1, device_id={"tm": other}, device_id_type=MESH)

            count = count + there.astype(jnp.int32)
    for d in range(1, size):
        pl.semaphore_signal(
            barrier, inc=1, device_id={"swath": (place + d) % size}, device_id_type=MESH
        )
    return barrier, count


def pick(weighted, routes_ref, counts_ref, owner, slot):
    block_count = routes_ref.shape[1]
    place = jnp.int32(0)
    chosen = jnp.full((), -1, jnp.int32)
    for r in range(block_count):
        named = routes_ref[0, r] == owner
        live = r < counts_ref[0, 0]
        chosen = jnp.where(named & live & (place == slot), r, chosen)
        place = place + named.astype(jnp.int32)
    block = jnp.zeros(weighted[0].shape, jnp.float32)
    for r in range(block_count):
        block = jnp.where(chosen == r, weighted[r], block)
    return block.astype(jnp.bfloat16)


def kernel(times, size, total_slots, block_rows, design_ref, process_ref, prior_ref, routes_ref,
           counts_ref, out_diag_ref, out_coup_ref, skew, obs, proc, leaving, prior, work, high, low,
           right_high, right_low, solved_high, solved_low, parts, shares, land, terms, cross, corner,
           last_cross, last_full, last_half, first_send, first_recv, spread_send, spread_recv,
           prior_send, prior_recv, inner_send, inner_recv, term_send, term_recv, cross_send, cross_recv, share_send,
           share_recv, part_send, part_recv, last_send, last_recv):
    place, me = lax.axis_index("swath"), lax.axis_index("tm")
    rows, order = process_ref.shape
    block_count = routes_ref.shape[1]
    slot_count = block_count // 2
    reach, half = size // 2, rows // 2
    hops = size - 1
    barrier, count = greet(times, size, place, me)

    behind, ahead = me >= 1, me + 1 < times
    other = flipped(place, reach)
    spread = lambda view, k, own=None: Spread(
        size, place, view, spread_send, spread_recv, k * hops, own
    )
    inner = lambda view, k: Spread(reach, place, view, inner_send, inner_recv, k * (reach - 1))
    slots = [pl.ds(c * block_rows, block_rows) for c in range(slot_count)]
    far_move = lambda source, target, k: Move(
        source, target, first_send, first_recv, k, me + 1, ahead, behind
    )
    far_moves = [
        far_move(process_ref, proc.at[1, place], 0),
        far_move(proc.at[0, other], proc.at[1, other], 1),
    ]
    for c, cut in enumerate(slots):
        far_moves.append(far_move(leaving.at[cut], obs.at[1, place, cut], c + 2))
    near_proc = spread(lambda held: proc.at[0, held], 0, process_ref)
    near_prior = Spread(size, place, lambda held: prior.at[held], prior_send, prior_recv)
    near_obs = spread(lambda held: obs.at[0, held], 1)
    far_procs = [
        inner(lambda held: proc.at[1, held], 0),
        inner(lambda held: proc.at[1, flipped(held, reach)], 1),
    ]
    far_obs = [
        spread(lambda held, cut=cut: obs.at[1, held, cut], 2 + c) for c, cut in enumerate(slots)
    ]
    prior[place] = jnp.broadcast_to(prior_ref[...], prior.shape[1:])
    pl.semaphore_wait(barrier, count)
    far_moves[0].start()
    near_proc.start_own()
    proc[0, place] = process_ref[...]

    weighted = []
    for r in range(block_count):
        raw = design_ref[r * block_rows : (r + 1) * block_rows, :].astype(jnp.float32)
        mean_sq = jnp.mean(raw * raw, axis=-1, keepdims=True)
        weighted.append(raw * lax.rsqrt(4.0 * total_slots * (mean_sq + 1e-06)))
    for slot in range(slot_count):
        cut = slice(slot * block_rows, (slot + 1) * block_rows)
        obs[0, place, cut, :] = pick(weighted, routes_ref, counts_ref, me, slot)
    near_obs.start_own()
    for slot in range(slot_count):
        cut = slice(slot * block_rows, (slot + 1) * block_rows)
        leaving[cut, :] = pick(weighted, routes_ref, counts_ref, me + 1, slot)
        far_moves[slot + 2].start()
    near_prior.start_own()
    near_proc.forward()
    far_moves[1].start()
    far_moves[0].receive()
    far_procs[0].start_own()
    near_prior.forward()
    for c in range(slot_count):
        far_moves[c + 2].receive()
        far_obs[c].start_own()
    near_obs.forward()
    near_proc.finish()
    near_prior.finish()
    near_obs.finish()
    far_moves[1].receive()
    far_procs[1].start_own()

    def gram(which, cut, b):
        total = None
        for i in range(size):
            term = lax.dot_general(
                obs[which, i, cut, b * rows : (b + 1) * rows],
                obs[which, i, cut, b * rows :],
                (((0,), (0,)), ((), ())),
                preferred_element_type=jnp.float32,
            )
            total = term if total is None else total + term
        return total

    square = (rows, rows)
    unit = lax.broadcasted_iota(jnp.int32, square, 0) == lax.broadcasted_iota(jnp.int32, square, 1)
    cuts = [slice(b * rows, (b + 1) * rows) for b in range(size)]
    for b in range(size):
        work[b, :, b * rows :] = gram(0, slice(None), b)
        work[b, :, cuts[b]] += jnp.where(unit, jnp.broadcast_to(prior[b][:1], square), 0.0)
        right_high[cuts[b], :order] = proc[0, b]
    for one in far_procs:
        one.forward()
        one.finish()
    both = lambda a, b: proc[0, a, :, cuts[b]].astype(jnp.float32) + proc[1, a, :, cuts[b]].astype(
        jnp.float32
    )
    for b in range(size):
        for q in range(size):
            right_high[cuts[b], order + q * rows : order + (q + 1) * rows] = proc[1, q, :, cuts[b]].T
            if q >= b:
                work[b, :, cuts[q]] += 0.5 * (both(b, q) + both(q, b).T)
    for c in range(slot_count):
        far_obs[c].forward()
        far_obs[c].finish()
        for b in range(size):
            work[b, :, b * rows :] += gram(1, slots[c], b)
    for s in range(size):

        @pl.when(place == s)
        def _():
            for d in range(reach):
                q = (s + d) % size
                block = work[s, :, cuts[q]] if q >= s else work[q, :, cuts[s]].T
                shares[0, s, d * rows : (d + 1) * rows] = block
            a, h = s % reach, s // reach
            shares[0, s, reach * rows :] = work[a, h * half : (h + 1) * half, cuts[a + reach]]

    piece = rows // size
    sending = []
    column = lambda part, b: pl.ds(pl.multiple_of(part * order + b * rows, rows), rows)
    share_cuts = [pl.ds(d * rows, rows) for d in range(reach)] + [pl.ds(reach * rows, half)]
    for level in range(LEVELS):
        distance = 2**level
        last = level == LEVELS - 1
        behind, ahead = me >= distance, me + distance < times
        if level == 0:
            factor(work, high, low)
        else:
            arrivals = parts.at[level - 1]
            below = 2 ** (level - 1)
            has_next = me + 2 * below <= times
            has_previous = me >= 2 * below

            part_spreads, part_moves = [], []
            for c in range(size):
                cut = pl.ds(c * piece, piece)
                index = ((level - 1) * size + c) * 2
                part_spreads.append(
                    Spread(
                        size, place, lambda held, cut=cut: arrivals.at[held, :, cut], part_send,
                        part_recv, ((level - 1) * size + c) * hops,
                    )
                )
                part_moves.append([
                    Move(cross.at[level - 1, k, cut], arrivals.at[place, k, cut], cross_send,
                         cross_recv, index + k, me, there, there)
                    for k, there in enumerate((has_next, has_previous))
                ])

            def beside(j, late):
                if late:
                    pl.when(j == 0)(pending)
                for c in range(size):
                    land_at, pass_at = PLAN[min(level, 2) - 1][c % 4]
                    if land_at % 2 == late:

                        @pl.when(j == land_at // 2)
                        def _():
                            for move in part_moves[c]:
                                move.receive()
                            part_spreads[c].start_own()

                    if pass_at % 2 == late:
                        pl.when(j == pass_at // 2)(part_spreads[c].forward)

            factor(work, high, low, beside)
            for c in range(size):
                if PLAN[min(level, 2) - 1][c % 4][1] >= 2 * size:
                    part_spreads[c].forward()
            for one in part_spreads:
                one.finish()
            sending += part_spreads
            for b in range(size):
                for part in range(2):
                    top, bottom = split(arrivals[b, part])
                    right_high[cuts[b], part * order : (part + 1) * order] = top
                    right_low[cuts[b], part * order : (part + 1) * order] = bottom

        goes_down = behind & (me + distance <= times)
        comes_down = me + 2 * distance <= times
        whole = lambda part: (
            solved_high[:, part * order : (part + 1) * order],
            solved_low[:, part * order : (part + 1) * order],
        )
        lower = None if level == 0 else right_low
        term_moves, turned = [None, None], [None, None]
        for part in (1, 0) if last else (0, 1):
            solve(high, low, right_high, lower, solved_high, solved_low, part, size)
            pair = lambda b, part=part: (solved_high[:, column(part, b)], solved_low[:, column(part, b)])
            own = pair(place)
            own = (own[0].T, own[1].T)
            turned[part] = own
            if last and part == 0:
                cross[level, 0] = joined(turned[1], whole(0), (1, 0))
                final = Move(
                    cross.at[level, 0], last_cross, last_send, last_recv, 0, me - distance, goes_down,
                    comes_down,
                )
                final.start()
            wide = [pair((place + d) % size) for d in range(reach)]
            wide = tuple(jnp.concatenate([w[k] for w in wide], axis=1) for k in range(2))
            product = joined(own, wide, (1, 0))
            for d in range(reach):
                terms[level, part, d * rows : (d + 1) * rows] = product[:, d * rows : (d + 1) * rows]
            a, h = place % reach, place // reach
            first = pair(a)
            corner[...] = joined((first[0].T, first[1].T), pair(a + reach), (1, 0))
            terms[level, part, reach * rows :] = corner[pl.ds(pl.multiple_of(h * half, half), half), :]
            sends, receives = (ahead, behind) if part == 0 else (behind, ahead)
            moves = []
            for d, cut in enumerate(share_cuts):
                move = Move(
                    terms.at[level, part, cut], land.at[level, part, cut], term_send, term_recv,
                    (level * 2 + part) * len(share_cuts) + d,
                    me + distance if part == 0 else me - distance, sends, receives,
                )
                move.start()
                moves.append(move)
            term_moves[part] = moves

        cross_moves = []
        if not last:
            cross[level, 0] = joined(turned[1], whole(0), (1, 0))
            cross[level, 1] = joined(turned[0], whole(1), (1, 0))
            target = parts.at[level]
            for c in range(size):
                cut = pl.ds(c * piece, piece)
                index = (level * size + c) * 2
                cross_moves.append(
                    Move(cross.at[level, 0, cut], target.at[place, 0, cut], cross_send, cross_recv,
                         index, me - distance, goes_down, comes_down)
                )
                cross_moves.append(
                    Move(cross.at[level, 1, cut], target.at[place, 1, cut], cross_send, cross_recv,
                         index + 1, me + distance, behind & ahead, me >= 2 * distance)
                )
            for move in cross_moves:
                move.start()

        spreads = []
        for d, cut in enumerate(share_cuts):
            term_moves[0][d].receive()
            term_moves[1][d].receive()
            shares[level + 1, place, cut] = (
                shares[level, place, cut] - land[level, 0, cut] - land[level, 1, cut]
            )
            if not last:
                spreads.append(
                    Spread(size, place, lambda held, cut=cut: shares.at[level + 1, held, cut],
                           share_send, share_recv, (level * len(share_cuts) + d) * hops)
                )
                spreads[-1].start_own()
                if d == len(share_cuts) - 2:
                    spreads[0].forward()
        sending += term_moves[0] + term_moves[1] + cross_moves + spreads
        if level == 0:
            mine = pl.ds(pl.multiple_of(place * rows, rows), rows)
            for q in range(size):
                there = proc[0, q, :, mine].astype(jnp.float32) + proc[1, q, :, mine].astype(jnp.float32)
                here = proc[0, place, :, cuts[q]].astype(jnp.float32) + proc[
                    1, place, :, cuts[q]
                ].astype(jnp.float32)
                skew[:, cuts[q]] = 0.5 * (here - there.T)
        if not last:
            spreads[0].finish()
            held = shares.at[level + 1]
            for s in range(size):
                work[s, :, cuts[s]] = held[s, :rows]

            def pending(spreads=spreads, held=held):
                for one in spreads[1:]:
                    one.forward()
                for one in spreads[1:]:
                    one.finish()
                for s in range(size):
                    for d in range(1, reach):
                        q = (s + d) % size
                        block = held[s, d * rows : (d + 1) * rows]
                        if q >= s:
                            work[s, :, cuts[q]] = block
                        else:
                            work[q, :, cuts[s]] = block.T
                    a, h = s % reach, s // reach
                    work[a, h * half : (h + 1) * half, cuts[a + reach]] = held[s, reach * rows :]

    copies = []
    for d in range(1, reach):
        copies.append(
            pltpu.make_async_remote_copy(
                src_ref=shares.at[LEVELS, place, share_cuts[d]],
                dst_ref=last_full.at[d - 1],
                send_sem=last_send.at[d],
                recv_sem=last_recv.at[d],
                device_id={"swath": (place + d) % size},
                device_id_type=MESH,
            )
        )
    copies.append(
        pltpu.make_async_remote_copy(
            src_ref=shares.at[LEVELS, place, share_cuts[reach]],
            dst_ref=last_half,
            send_sem=last_send.at[reach],
            recv_sem=last_recv.at[reach],
            device_id={"swath": (place + reach) % size},
            device_id_type=MESH,
        )
    )
    for copy in copies:
        copy.start()
    final.receive()
    out_coup_ref[...] = last_cross[...]
    for copy in copies:
        copy.wait_recv()
    for s in range(size):

        @pl.when(place == s)
        def _():
            own = shares.at[LEVELS, s]
            for d in range(reach):
                q = (s + d) % size
                out_diag_ref[:, cuts[q]] = own[d * rows : (d + 1) * rows]
            for d in range(1, reach):
                q = (s - d) % size
                out_diag_ref[:, cuts[q]] = last_full[d - 1].T
            pieces = [own[reach * rows :], last_half[...]]
            if s < reach:
                block = jnp.concatenate(pieces, axis=0)
            else:
                block = jnp.concatenate(pieces[::-1], axis=0).T
            q = (s + reach) % size
            out_diag_ref[:, cuts[q]] = block

    for copy in copies:
        copy.wait_send()
    final.sent()
    for move in far_moves + sending:
        move.sent()
    for one in [near_proc, near_prior, near_obs] + far_procs + far_obs:
        one.sent()


def shards(design, process, prior_prec, routes, counts):
    times, size = lax.axis_size("tm"), lax.axis_size("swath")
    rows, order = process.shape[1:]
    block_count = routes.shape[1]
    block_rows = design.shape[1] // block_count
    slot_count = block_count // 2
    observed = slot_count * block_rows
    total_slots = 2 * observed * size
    share = rows * (size // 2) + rows // 2
    hops = size - 1
    kinds = size // 2 + 1
    vmem, smem = (pl.BlockSpec(memory_space=m) for m in (pltpu.VMEM, pltpu.SMEM))
    f32, bf16 = jnp.float32, jnp.bfloat16
    dma = lambda n: [pltpu.SemaphoreType.DMA((n,))] * 2
    diag_rows, coup_rows, skew = pl.pallas_call(
        functools.partial(kernel, times, size, total_slots, block_rows),
        out_shape=(jax.ShapeDtypeStruct((rows, order), f32),) * 3,
        in_specs=[vmem, vmem, vmem, smem, smem],
        out_specs=(vmem,) * 3,
        scratch_shapes=[
            pltpu.VMEM((2, size, observed, order), bf16),
            pltpu.VMEM((2, size, rows, order), bf16),
            pltpu.VMEM((observed, order), bf16),
            pltpu.VMEM((size, 8, rows), f32),
            pltpu.VMEM((size, rows, order), f32),
            pltpu.VMEM((order, order), bf16),
            pltpu.VMEM((order, order), bf16),
            pltpu.VMEM((order, 2 * order), bf16),
            pltpu.VMEM((order, 2 * order), bf16),
            pltpu.VMEM((order, 2 * order), bf16),
            pltpu.VMEM((order, 2 * order), bf16),
            pltpu.VMEM((LEVELS - 1, size, 2, rows, order), f32),
            pltpu.VMEM((LEVELS + 1, size, share, rows), f32),
            pltpu.VMEM((LEVELS, 2, share, rows), f32),
            pltpu.VMEM((LEVELS, 2, share, rows), f32),
            pltpu.VMEM((LEVELS, 2, rows, order), f32),
            pltpu.VMEM((rows, rows), f32),
            pltpu.VMEM((rows, order), f32),
            pltpu.VMEM((max(size // 2 - 1, 1), rows, rows), f32),
            pltpu.VMEM((rows // 2, rows), f32),
        ]
        + dma(2 + slot_count)
        + dma((2 + slot_count) * hops)
        + dma(hops)
        + dma(2 * (size // 2 - 1))
        + dma(LEVELS * 2 * kinds)
        + dma((LEVELS - 1) * size * 2)
        + dma((LEVELS - 1) * kinds * hops)
        + dma((LEVELS - 1) * size * hops)
        + dma(kinds),
        compiler_params=pltpu.CompilerParams(collective_id=0, has_side_effects=True),
    )(design[0], process[0], prior_prec, routes, counts)
    return ((diag_rows + skew)[None], -coup_rows[None])


def solution(mesh):
    return jax.shard_map(
        shards,
        mesh=mesh,
        in_specs=(
            P("tm", "swath", None),
            P("tm", "swath", None),
            P("tm", "swath"),
            P("tm", "swath"),
            P("tm", "swath"),
        ),
        out_specs=(P("tm", "swath", None), P("tm", "swath", None)),
        check_vma=False,
    )
```

```python
import functools

import jax
import jax.numpy as jnp
from jax import lax
from jax.experimental import pallas as pl
from jax.experimental.pallas import tpu as pltpu
from jax.sharding import PartitionSpec as P

LEVELS = 3
W = 8
SHARES = ((5, 5, 4, 2), (3, 5, 4, 4))
PLAN = (
    ((1, 3, 3, 6), (2, 4, 4, 7), (3, 5, 5, 8), (3, 5, 6, 8)),
    ((0, 3), (1, 5), (2, 6), (3, 7)),
)
MESH = pl.DeviceIdType.MESH


def split(x):
    high = x.astype(jnp.bfloat16)
    return high, (x - high.astype(jnp.float32)).astype(jnp.bfloat16)

def joined(a, b, dims):
    (ah, al), (bh, bl) = a, b
    return lax.dot_general(
        jnp.concatenate([ah, ah, al], axis=dims[0]),
        jnp.concatenate([bh, bl, bh], axis=dims[1]),
        (((dims[0],), (dims[1],)), ((), ())),
        preferred_element_type=jnp.float32,
    )

def pivots(columns):
    spread = lambda x: jnp.broadcast_to(x, columns[0].shape)
    entry = {(k, s): spread(columns[s][k : k + 1, :]) for s in range(W) for k in range(s, W)}
    scale, lower = [], {}
    for s in range(W):
        pivot = entry[s, s]
        turned = 1.0 / pivot
        scale.append(lax.rsqrt(pivot))
        if s + 1 < W:
            near = entry[s + 1, s]
            entry[s + 1, s + 1] = entry[s + 1, s + 1] - (near * near) * turned
        for k in range(s + 1, W):
            lower[k, s] = entry[k, s] * scale[s]
        for k in range(s + 2, W):
            part = entry[k, s] * turned
            for t in range(s + 1, k + 1):
                entry[k, t] = entry[k, t] - part * entry[t, s]
    return scale, lower

def forward(values, scale, lower):
    out = []
    values = list(values)
    for s in range(W):
        out.append(values[s] * scale[s])
        for k in range(s + 1, W):
            values[k] = values[k] - lower[k, s] * out[s]
    return out

def factor_inverse(m, panel=32):
    n = m.shape[0]
    rows = [m[W * g : W * (g + 1), :] for g in range(n // W)]
    lane = lax.broadcasted_iota(jnp.int32, (W, n), 1)
    sub = lax.broadcasted_iota(jnp.int32, (W, n), 0)
    spread = lambda x: jnp.broadcast_to(x, (W, n))
    cleared = lambda x, first: jnp.where((lane >= first) & (lane < first + W), 0.0, x)
    column = lambda h, first: [spread(rows[h][:, first + s : first + s + 1]) for s in range(W)]

    def solve_rows(row, first, scale, lower):
        row = cleared(row, first)
        start = [jnp.where(lane == first + s, 1.0, spread(row[s : s + 1, :])) for s in range(W)]
        solved = forward(start, scale, lower)
        group = solved[0]
        for s in range(1, W):
            group = jnp.where(sub == s, solved[s], group)
        return solved, group

    def take(row, factors, solved, first):
        row = cleared(row, first)
        for s in range(W):
            row = row - factors[s] * solved[s]
        return row

    per = panel // W
    for p in range(n // panel):
        end = (p + 1) * per
        for q in range(0, per, 2):
            g, h = p * per + q, p * per + q + 1
            first, second = g * W, h * W
            scale, lower = pivots(column(g, first))
            cross = forward(column(h, first), scale, lower)
            crossed = {(k, s): spread(cross[s][k : k + 1, :]) for s in range(W) for k in range(W)}
            corner = column(h, second)
            for t in range(W):
                for s in range(W):
                    corner[t] = corner[t] - cross[s] * crossed[t, s]
            scale2, lower2 = pivots(corner)
            others = range(h + 1, end)
            left = {i: column(i, first) for i in others}
            right = {i: column(i, second) for i in others}
            solved, group = solve_rows(rows[g], first, scale, lower)
            rows[g] = group
            solved2, group2 = solve_rows(take(rows[h], cross, solved, first), second, scale2, lower2)
            rows[h] = group2
            for i in others:
                one = forward(left[i], scale, lower)
                two = right[i]
                for t in range(W):
                    for s in range(W):
                        two[t] = two[t] - one[s] * crossed[t, s]
                two = forward(two, scale2, lower2)
                rows[i] = take(take(rows[i], one, solved, first), two, solved2, second)
        if end < n // W:
            edge = end * W
            kept = lambda g: jnp.where((lane < (g + 1) * W) | (lane >= edge), rows[g], 0.0)
            done = jnp.concatenate([kept(g) for g in range(p * per, end)], axis=0)
            pair = split(done)
            term = joined(pair, pair, (0, 0))
            outside = (lane < p * panel) | (lane >= (p + 1) * panel)
            for i in range(end, n // W):
                rows[i] = jnp.where(outside, rows[i], 0.0) - term[W * i : W * (i + 1), :]
    out = jnp.concatenate(rows, axis=0)
    down = lax.broadcasted_iota(jnp.int32, (n, n), 0)
    across = lax.broadcasted_iota(jnp.int32, (n, n), 1)
    return jnp.where(down >= across, out, 0.0)


def plain(a, b, dims):
    return lax.dot_general(
        a, b, (((dims[0],), (dims[1],)), ((), ())), preferred_element_type=jnp.float32
    )


def factor(work, high, low, beside=None):
    blocks, rows, order = work.shape
    down = lax.broadcasted_iota(jnp.int32, (rows, rows), 0)
    across = lax.broadcasted_iota(jnp.int32, (rows, rows), 1)
    unit = jnp.where(down == across, 1.0, 0.0)
    column_block = lax.broadcasted_iota(jnp.int32, (rows, order), 1) // rows

    def step(j, carry):
        at = pl.ds(pl.multiple_of(j * rows, rows), rows)
        if beside is not None:
            beside(j, 0)
        inverse = factor_inverse(work[j, :, at])
        if beside is not None:
            beside(j, 1)
        work[j, :, at] = unit
        solved = joined(split(inverse), split(work[j]), (1, 0))
        solved_high, solved_low = split(solved)
        high[at, :] = solved_high
        low[at, :] = solved_low
        for i in range(1, blocks):

            @pl.when(i > j)
            def _():
                cut = slice(i * rows, (i + 1) * rows)
                left = (high[at, cut].T, low[at, cut].T)
                work[i, :, at] = jnp.zeros((rows, rows), jnp.float32)
                work[i] = work[i] - joined(left, (solved_high, solved_low), (1, 0))

        keep = column_block <= j
        high[at, :] = jnp.where(keep, solved_high, 0.0).astype(jnp.bfloat16)
        low[at, :] = jnp.where(keep, solved_low, 0.0).astype(jnp.bfloat16)
        return carry

    lax.fori_loop(0, blocks, step, 0)


def solve(high, low, right_high, right_low, out_high, out_low, part, blocks, turn):
    order = high.shape[0]
    rows = order // blocks
    across = slice(part * order, (part + 1) * order)
    for j in range(blocks):
        at, deep = slice(j * rows, (j + 1) * rows), (j + 1) * rows
        left = (high[at, :deep], low[at, :deep])
        at_right = (slice(None), slice(part * order, part * order + deep)) if turn else (slice(deep), across)
        dims = (1, 1) if turn else (1, 0)
        if right_low is None:
            solved = plain(left[0], right_high[at_right], dims) + plain(left[1], right_high[at_right], dims)
        else:
            solved = joined(left, (right_high[at_right], right_low[at_right]), dims)
        solved_high, solved_low = split(solved)
        out_high[at, across] = solved_high
        out_low[at, across] = solved_low


def flipped(place, bit):
    return place + bit - 2 * bit * ((place // bit) % 2)


class Spread:
    def __init__(self, size, place, view, send_sem, recv_sem, base=0, own=None):
        bits = [size >> (k + 1) for k in range(size.bit_length() - 1)]
        self.plan = [(b, 0) for b in bits]
        for k, b in enumerate(bits):
            earlier = [0]
            for e in bits[:k]:
                earlier += [m + e for m in earlier]
            self.plan += [(b, m) for m in earlier if m]
        self.source = {}
        for b, m in self.plan:
            if m:
                last = m & -m
                self.source[b, m] = self.plan.index((last, m - last))
        self.copies = []
        for k, (b, m) in enumerate(self.plan):
            held = place
            for e in bits:
                if m & e:
                    held = flipped(held, e)
            self.copies.append(
                pltpu.make_async_remote_copy(
                    src_ref=own if own is not None and m == 0 else view(held),
                    dst_ref=view(held),
                    send_sem=send_sem.at[base + k],
                    recv_sem=recv_sem.at[base + k],
                    device_id={"swath": flipped(place, b)},
                    device_id_type=MESH,
                )
            )

    def start_own(self):
        for copy, (b, m) in zip(self.copies, self.plan):
            if m == 0:
                copy.start()

    def forward(self):
        waited = set()
        for copy, item in zip(self.copies, self.plan):
            if item in self.source:
                source = self.source[item]
                if source not in waited:
                    self.copies[source].wait_recv()
                    waited.add(source)
                copy.start()

    def finish(self):
        waited = set(self.source.values())
        for k, copy in enumerate(self.copies):
            if k not in waited:
                copy.wait_recv()

    def sent(self):
        for copy in self.copies:
            copy.wait_send()


class Move:
    def __init__(self, source, target, send_sem, recv_sem, index, device, sends, receives):
        self.copy = pltpu.make_async_remote_copy(
            src_ref=source,
            dst_ref=target,
            send_sem=send_sem.at[index],
            recv_sem=recv_sem.at[index],
            device_id={"tm": device},
            device_id_type=MESH,
        )
        self.target, self.sends, self.receives = target, sends, receives

    def start(self):
        pl.when(self.sends)(self.copy.start)

    def receive(self):
        pl.when(self.receives)(self.copy.wait_recv)

        @pl.when(jnp.logical_not(self.receives))
        def _():
            self.target[...] = jnp.zeros(self.target.shape, self.target.dtype)

    def sent(self):
        pl.when(self.sends)(self.copy.wait_send)


def band_cuts(rows, count, level):
    shares = SHARES[min(level, 1)] if count == 4 else (16 // count,) * count
    sizes = [rows * share // 16 for share in shares]
    return [pl.ds(sum(sizes[:c]), size) for c, size in enumerate(sizes)]


def greet(times, size, place, me):
    barrier = pltpu.get_barrier_semaphore()
    count = jnp.int32(size - 1)
    for level in range(LEVELS):
        distance = 2**level
        for there, other in ((me >= distance, me - distance), (me + distance < times, me + distance)):

            @pl.when(there)
            def _():
                pl.semaphore_signal(barrier, inc=1, device_id={"tm": other}, device_id_type=MESH)

            count = count + there.astype(jnp.int32)
    for d in range(1, size):
        pl.semaphore_signal(
            barrier, inc=1, device_id={"swath": (place + d) % size}, device_id_type=MESH
        )
    return barrier, count


def pick(weighted, routes_ref, counts_ref, owner, slot):
    block_count = routes_ref.shape[1]
    place = jnp.int32(0)
    chosen = jnp.full((), -1, jnp.int32)
    for r in range(block_count):
        named = routes_ref[0, r] == owner
        live = r < counts_ref[0, 0]
        chosen = jnp.where(named & live & (place == slot), r, chosen)
        place = place + named.astype(jnp.int32)
    block = jnp.zeros(weighted[0].shape, jnp.float32)
    for r in range(block_count):
        block = jnp.where(chosen == r, weighted[r], block)
    return block.astype(jnp.bfloat16)


def kernel(times, size, total_slots, block_rows, design_ref, process_ref, prior_ref, routes_ref,
           counts_ref, out_diag_ref, out_coup_ref, skew, obs, proc, leaving, prior, work, high, low,
           right_high, right_low, solved_high, solved_low, parts, shares, land, terms, cross, corner,
           last_cross, last_full, last_half, first_send, first_recv, spread_send, spread_recv,
           prior_send, prior_recv, inner_send, inner_recv, term_send, term_recv, cross_send, cross_recv, share_send,
           share_recv, part_send, part_recv, relay_send, relay_recv, again_send, again_recv, last_send, last_recv):
    place, me = lax.axis_index("swath"), lax.axis_index("tm")
    rows, order = process_ref.shape
    block_count = routes_ref.shape[1]
    slot_count = block_count // 2
    reach, half = size // 2, rows // 2
    hops = size - 1
    barrier, count = greet(times, size, place, me)

    behind, ahead = me >= 1, me + 1 < times
    other = flipped(place, reach)
    spread = lambda view, k, own=None: Spread(
        size, place, view, spread_send, spread_recv, k * hops, own
    )
    inner = lambda view, k: Spread(reach, place, view, inner_send, inner_recv, k * (reach - 1))
    slots = [pl.ds(c * block_rows, block_rows) for c in range(slot_count)]
    far_move = lambda source, target, k: Move(
        source, target, first_send, first_recv, k, me + 1, ahead, behind
    )
    far_moves = [
        far_move(process_ref, proc.at[1, place], 0),
        far_move(proc.at[0, other], proc.at[1, other], 1),
    ]
    for c, cut in enumerate(slots):
        far_moves.append(far_move(leaving.at[cut], obs.at[1, place, cut], c + 2))
    near_proc = spread(lambda held: proc.at[0, held], 0, process_ref)
    near_prior = Spread(size, place, lambda held: prior.at[held], prior_send, prior_recv)
    near_obs = spread(lambda held: obs.at[0, held], 1)
    far_procs = [
        inner(lambda held: proc.at[1, held], 0),
        inner(lambda held: proc.at[1, flipped(held, reach)], 1),
    ]
    far_obs = [
        spread(lambda held, cut=cut: obs.at[1, held, cut], 2 + c) for c, cut in enumerate(slots)
    ]
    prior[place] = jnp.broadcast_to(prior_ref[...], prior.shape[1:])
    pl.semaphore_wait(barrier, count)
    far_moves[0].start()
    near_proc.start_own()
    proc[0, place] = process_ref[...]

    weighted = []
    for r in range(block_count):
        raw = design_ref[r * block_rows : (r + 1) * block_rows, :].astype(jnp.float32)
        mean_sq = jnp.mean(raw * raw, axis=-1, keepdims=True)
        weighted.append(raw * lax.rsqrt(4.0 * total_slots * (mean_sq + 1e-06)))
    for slot in range(slot_count):
        cut = slice(slot * block_rows, (slot + 1) * block_rows)
        obs[0, place, cut, :] = pick(weighted, routes_ref, counts_ref, me, slot)
    near_obs.start_own()
    for slot in range(slot_count):
        cut = slice(slot * block_rows, (slot + 1) * block_rows)
        leaving[cut, :] = pick(weighted, routes_ref, counts_ref, me + 1, slot)
        far_moves[slot + 2].start()
    near_prior.start_own()
    near_proc.forward()
    far_moves[1].start()
    far_moves[0].receive()
    far_procs[0].start_own()
    near_prior.forward()
    for c in range(slot_count):
        far_moves[c + 2].receive()
        far_obs[c].start_own()
    near_obs.forward()
    near_proc.finish()
    near_prior.finish()
    near_obs.finish()

    def gram(which, cut, b):
        total = None
        for i in range(size):
            term = lax.dot_general(
                obs[which, i, cut, b * rows : (b + 1) * rows],
                obs[which, i, cut, b * rows :],
                (((0,), (0,)), ((), ())),
                preferred_element_type=jnp.float32,
            )
            total = term if total is None else total + term
        return total

    square = (rows, rows)
    unit = lax.broadcasted_iota(jnp.int32, square, 0) == lax.broadcasted_iota(jnp.int32, square, 1)
    cuts = [slice(b * rows, (b + 1) * rows) for b in range(size)]
    for b in range(size):
        work[b, :, b * rows :] = gram(0, slice(None), b)
        work[b, :, cuts[b]] += jnp.where(unit, jnp.broadcast_to(prior[b][:1], square), 0.0)
        right_high[cuts[b], :order] = proc[0, b]
    far_moves[1].receive()
    far_procs[1].start_own()
    far_obs[0].forward()
    for one in far_procs:
        one.forward()
        one.finish()
    both = lambda a, b: proc[0, a, :, cuts[b]].astype(jnp.float32) + proc[1, a, :, cuts[b]].astype(
        jnp.float32
    )
    for b in range(size):
        right_high[cuts[b], order:] = proc[1, b]
        for q in range(size):
            if q >= b:
                work[b, :, cuts[q]] += 0.5 * (both(b, q) + both(q, b).T)
    for c in range(slot_count):
        far_obs[c].finish()
        if c + 1 < slot_count:
            far_obs[c + 1].forward()
        for b in range(size):
            work[b, :, b * rows :] += gram(1, slots[c], b)
    for s in range(size):

        @pl.when(place == s)
        def _():
            for d in range(reach):
                q = (s + d) % size
                block = work[s, :, cuts[q]] if q >= s else work[q, :, cuts[s]].T
                shares[0, s, d * rows : (d + 1) * rows] = block
            a, h = s % reach, s // reach
            shares[0, s, reach * rows :] = work[a, h * half : (h + 1) * half, cuts[a + reach]]

    bands = [band_cuts(rows, size, level) for level in range(LEVELS)]
    sending = []
    column = lambda part, b: pl.ds(pl.multiple_of(part * order + b * rows, rows), rows)
    share_cuts = [pl.ds(d * rows, rows) for d in range(reach)] + [pl.ds(reach * rows, half)]
    for level in range(LEVELS):
        distance = 2**level
        last = level == LEVELS - 1
        behind, ahead = me >= distance, me + distance < times
        if level == 0:
            factor(work, high, low)
        else:
            arrivals = parts.at[level - 1]
            below = 2 ** (level - 1)
            has_next = me + 2 * below <= times
            has_previous = me >= 2 * below

            part_spreads, relays, actions = [], [], [(1, pending)]
            for c in range(size):
                cut = bands[level - 1][c]
                base = ((level - 1) * size + c) * hops
                kinds = (has_next, has_previous)
                arrive = [
                    Move(cross.at[level - 1, k, cut], arrivals.at[place, k, cut], cross_send,
                         cross_recv, ((level - 1) * size + c) * 2 + k, me, kinds[k], kinds[k])
                    for k in range(2)
                ]
                if level == 1:
                    relay = Move(
                        arrivals.at[place, 0, cut], arrivals.at[place, 1, cut], relay_send, relay_recv,
                        c, me + 2 * below, me + 2 * below < times, has_previous,
                    )
                    pair_of = [
                        Spread(size, place, lambda held, cut=cut, k=k: arrivals.at[held, k, cut],
                               sems[0], sems[1], first)
                        for k, sems, first in (
                            (0, (part_send, part_recv), base),
                            (1, (again_send, again_recv), c * hops),
                        )
                    ]

                    def landed(arrive=arrive, relay=relay, pair_of=pair_of):
                        arrive[0].receive()
                        relay.start()
                        pair_of[0].start_own()

                    def relayed(relay=relay, pair_of=pair_of):
                        relay.receive()
                        pair_of[1].start_own()

                    steps = (landed, pair_of[0].forward, relayed, pair_of[1].forward)
                    relays.append(relay)
                else:
                    pair_of = [
                        Spread(size, place, lambda held, cut=cut: arrivals.at[held, :, cut], part_send,
                               part_recv, base)
                    ]

                    def landed(arrive=arrive, pair_of=pair_of):
                        for move in arrive:
                            move.receive()
                        pair_of[0].start_own()

                    steps = (landed, pair_of[0].forward)
                part_spreads += pair_of
                actions += list(zip(PLAN[min(level, 2) - 1][c % 4], steps))
            actions.sort(key=lambda item: item[0])

            def beside(j, late):
                for point, act in actions:
                    if point % 2 == late and point < 2 * size:
                        pl.when(j == point // 2)(act)

            factor(work, high, low, beside)
            for point, act in actions:
                if point >= 2 * size:
                    act()
            for one in part_spreads:
                one.finish()
            sending += part_spreads + relays
            for b in range(size):
                for part in range(2):
                    top, bottom = split(arrivals[b, part])
                    right_high[cuts[b], part * order : (part + 1) * order] = top
                    right_low[cuts[b], part * order : (part + 1) * order] = bottom

        goes_down = behind & (me + distance <= times)
        comes_down = me + 2 * distance <= times
        whole = lambda part: (
            solved_high[:, part * order : (part + 1) * order],
            solved_low[:, part * order : (part + 1) * order],
        )
        lower = None if level == 0 else right_low
        term_moves, turned = [None, None], [None, None]
        for part in (1, 0) if last else (0, 1):
            turn = part == 1 and level < 2
            solve(high, low, right_high, lower, solved_high, solved_low, part, size, turn)
            pair = lambda b, part=part: (solved_high[:, column(part, b)], solved_low[:, column(part, b)])
            own = pair(place)
            own = (own[0].T, own[1].T)
            turned[part] = own
            if last and part == 0:
                cross[level, 0] = joined(turned[1], whole(0), (1, 0))
                final = Move(
                    cross.at[level, 0], last_cross, last_send, last_recv, 0, me - distance, goes_down,
                    comes_down,
                )
                final.start()
            wide = [pair((place + d) % size) for d in range(reach)]
            wide = tuple(jnp.concatenate([w[k] for w in wide], axis=1) for k in range(2))
            product = joined(own, wide, (1, 0))
            for d in range(reach):
                terms[level, part, d * rows : (d + 1) * rows] = product[:, d * rows : (d + 1) * rows]
            a, h = place % reach, place // reach
            first = pair(a)
            corner[...] = joined((first[0].T, first[1].T), pair(a + reach), (1, 0))
            terms[level, part, reach * rows :] = corner[pl.ds(pl.multiple_of(h * half, half), half), :]
            sends, receives = (ahead, behind) if part == 0 else (behind, ahead)
            moves = []
            for d, cut in enumerate(share_cuts):
                move = Move(
                    terms.at[level, part, cut], land.at[level, part, cut], term_send, term_recv,
                    (level * 2 + part) * len(share_cuts) + d,
                    me + distance if part == 0 else me - distance, sends, receives,
                )
                moves.append(move)
            moves[0].start()
            if last:
                for move in moves[1:]:
                    move.start()
            term_moves[part] = moves

        if not last:
            for d in range(1, len(share_cuts)):
                for part in range(2):
                    term_moves[part][d].start()

        cross_moves = []
        if not last:
            cross[level, 0] = joined(turned[1], whole(0), (1, 0))
            if level > 0:
                cross[level, 1] = joined(turned[0], whole(1), (1, 0))
            target = parts.at[level]
            for c in range(size):
                cut = bands[level][c]
                index = (level * size + c) * 2
                cross_moves.append(
                    Move(cross.at[level, 0, cut], target.at[place, 0, cut], cross_send, cross_recv,
                         index, me - distance, goes_down, comes_down)
                )
                if level == 0:
                    continue
                cross_moves.append(
                    Move(cross.at[level, 1, cut], target.at[place, 1, cut], cross_send, cross_recv,
                         index + 1, me + distance, behind & ahead, me >= 2 * distance)
                )
            for move in cross_moves:
                move.start()

        spreads = []
        for d, cut in enumerate(share_cuts):
            term_moves[0][d].receive()
            term_moves[1][d].receive()
            shares[level + 1, place, cut] = (
                shares[level, place, cut] - land[level, 0, cut] - land[level, 1, cut]
            )
            if not last:
                spreads.append(
                    Spread(size, place, lambda held, cut=cut: shares.at[level + 1, held, cut],
                           share_send, share_recv, (level * len(share_cuts) + d) * hops)
                )
                spreads[-1].start_own()
                if d == len(share_cuts) - 2:
                    spreads[0].forward()
        sending += term_moves[0] + term_moves[1] + cross_moves + spreads
        if level == 0:
            mine = pl.ds(pl.multiple_of(place * rows, rows), rows)
            for q in range(size):
                there = proc[0, q, :, mine].astype(jnp.float32) + proc[1, q, :, mine].astype(jnp.float32)
                here = proc[0, place, :, cuts[q]].astype(jnp.float32) + proc[
                    1, place, :, cuts[q]
                ].astype(jnp.float32)
                skew[:, cuts[q]] = 0.5 * (here - there.T)
        if not last:
            spreads[0].finish()
            held = shares.at[level + 1]
            for s in range(size):
                work[s, :, cuts[s]] = held[s, :rows]

            def pending(spreads=spreads, held=held):
                for one in spreads[1:]:
                    one.forward()
                for one in spreads[1:]:
                    one.finish()
                for s in range(size):
                    for d in range(1, reach):
                        q = (s + d) % size
                        block = held[s, d * rows : (d + 1) * rows]
                        if q >= s:
                            work[s, :, cuts[q]] = block
                        else:
                            work[q, :, cuts[s]] = block.T
                    a, h = s % reach, s // reach
                    work[a, h * half : (h + 1) * half, cuts[a + reach]] = held[s, reach * rows :]

    copies = []
    for d in range(1, reach):
        copies.append(
            pltpu.make_async_remote_copy(
                src_ref=shares.at[LEVELS, place, share_cuts[d]],
                dst_ref=last_full.at[d - 1],
                send_sem=last_send.at[d],
                recv_sem=last_recv.at[d],
                device_id={"swath": (place + d) % size},
                device_id_type=MESH,
            )
        )
    copies.append(
        pltpu.make_async_remote_copy(
            src_ref=shares.at[LEVELS, place, share_cuts[reach]],
            dst_ref=last_half,
            send_sem=last_send.at[reach],
            recv_sem=last_recv.at[reach],
            device_id={"swath": (place + reach) % size},
            device_id_type=MESH,
        )
    )
    for copy in copies:
        copy.start()
    final.receive()
    out_coup_ref[...] = last_cross[...]
    for copy in copies:
        copy.wait_recv()
    for s in range(size):

        @pl.when(place == s)
        def _():
            own = shares.at[LEVELS, s]
            for d in range(reach):
                q = (s + d) % size
                out_diag_ref[:, cuts[q]] = own[d * rows : (d + 1) * rows]
            for d in range(1, reach):
                q = (s - d) % size
                out_diag_ref[:, cuts[q]] = last_full[d - 1].T
            pieces = [own[reach * rows :], last_half[...]]
            if s < reach:
                block = jnp.concatenate(pieces, axis=0)
            else:
                block = jnp.concatenate(pieces[::-1], axis=0).T
            q = (s + reach) % size
            out_diag_ref[:, cuts[q]] = block

    for copy in copies:
        copy.wait_send()
    final.sent()
    for move in far_moves + sending:
        move.sent()
    for one in [near_proc, near_prior, near_obs] + far_procs + far_obs:
        one.sent()


def shards(design, process, prior_prec, routes, counts):
    times, size = lax.axis_size("tm"), lax.axis_size("swath")
    rows, order = process.shape[1:]
    block_count = routes.shape[1]
    block_rows = design.shape[1] // block_count
    slot_count = block_count // 2
    observed = slot_count * block_rows
    total_slots = 2 * observed * size
    share = rows * (size // 2) + rows // 2
    hops = size - 1
    kinds = size // 2 + 1
    vmem, smem = (pl.BlockSpec(memory_space=m) for m in (pltpu.VMEM, pltpu.SMEM))
    f32, bf16 = jnp.float32, jnp.bfloat16
    dma = lambda n: [pltpu.SemaphoreType.DMA((n,))] * 2
    diag_rows, coup_rows, skew = pl.pallas_call(
        functools.partial(kernel, times, size, total_slots, block_rows),
        out_shape=(jax.ShapeDtypeStruct((rows, order), f32),) * 3,
        in_specs=[vmem, vmem, vmem, smem, smem],
        out_specs=(vmem,) * 3,
        scratch_shapes=[
            pltpu.VMEM((2, size, observed, order), bf16),
            pltpu.VMEM((2, size, rows, order), bf16),
            pltpu.VMEM((observed, order), bf16),
            pltpu.VMEM((size, 8, rows), f32),
            pltpu.VMEM((size, rows, order), f32),
            pltpu.VMEM((order, order), bf16),
            pltpu.VMEM((order, order), bf16),
            pltpu.VMEM((order, 2 * order), bf16),
            pltpu.VMEM((order, 2 * order), bf16),
            pltpu.VMEM((order, 2 * order), bf16),
            pltpu.VMEM((order, 2 * order), bf16),
            pltpu.VMEM((LEVELS - 1, size, 2, rows, order), f32),
            pltpu.VMEM((LEVELS + 1, size, share, rows), f32),
            pltpu.VMEM((LEVELS, 2, share, rows), f32),
            pltpu.VMEM((LEVELS, 2, share, rows), f32),
            pltpu.VMEM((LEVELS, 2, rows, order), f32),
            pltpu.VMEM((rows, rows), f32),
            pltpu.VMEM((rows, order), f32),
            pltpu.VMEM((max(size // 2 - 1, 1), rows, rows), f32),
            pltpu.VMEM((rows // 2, rows), f32),
        ]
        + dma(2 + slot_count)
        + dma((2 + slot_count) * hops)
        + dma(hops)
        + dma(2 * (size // 2 - 1))
        + dma(LEVELS * 2 * kinds)
        + dma((LEVELS - 1) * size * 2)
        + dma((LEVELS - 1) * kinds * hops)
        + dma((LEVELS - 1) * size * hops)
        + dma(size)
        + dma(size * hops)
        + dma(kinds),
        compiler_params=pltpu.CompilerParams(collective_id=0, has_side_effects=True),
    )(design[0], process[0], prior_prec, routes, counts)
    return ((diag_rows + skew)[None], -coup_rows[None])


def solution(mesh):
    return jax.shard_map(
        shards,
        mesh=mesh,
        in_specs=(
            P("tm", "swath", None),
            P("tm", "swath", None),
            P("tm", "swath"),
            P("tm", "swath"),
            P("tm", "swath"),
        ),
        out_specs=(P("tm", "swath", None), P("tm", "swath", None)),
        check_vma=False,
    )
```

```python
import functools

import jax
import jax.numpy as jnp
from jax import lax
from jax.experimental import pallas as pl
from jax.experimental.pallas import tpu as pltpu
from jax.sharding import PartitionSpec as P

LEVELS = 3
W = 8
SHARES = ((5, 5, 4, 2), (3, 5, 4, 4))
POINTS = 5
PLAN = (
    ((2, 7, 7, 15), (4, 9, 9, 17), (7, 12, 12, 19), (7, 13, 13, 20)),
    ((0, 6), (0, 11), (2, 14), (4, 18)),
)
MESH = pl.DeviceIdType.MESH


def split(x):
    high = x.astype(jnp.bfloat16)
    return high, (x - high.astype(jnp.float32)).astype(jnp.bfloat16)

def joined(a, b, dims):
    (ah, al), (bh, bl) = a, b
    return lax.dot_general(
        jnp.concatenate([ah, ah, al], axis=dims[0]),
        jnp.concatenate([bh, bl, bh], axis=dims[1]),
        (((dims[0],), (dims[1],)), ((), ())),
        preferred_element_type=jnp.float32,
    )

def pivots(columns):
    spread = lambda x: jnp.broadcast_to(x, columns[0].shape)
    entry = {(k, s): spread(columns[s][k : k + 1, :]) for s in range(W) for k in range(s, W)}
    scale, lower = [], {}
    for s in range(W):
        pivot = entry[s, s]
        turned = 1.0 / pivot
        scale.append(lax.rsqrt(pivot))
        if s + 1 < W:
            near = entry[s + 1, s]
            entry[s + 1, s + 1] = entry[s + 1, s + 1] - (near * near) * turned
        for k in range(s + 1, W):
            lower[k, s] = entry[k, s] * scale[s]
        for k in range(s + 2, W):
            part = entry[k, s] * turned
            for t in range(s + 1, k + 1):
                entry[k, t] = entry[k, t] - part * entry[t, s]
    return scale, lower

def forward(values, scale, lower):
    out = []
    values = list(values)
    for s in range(W):
        out.append(values[s] * scale[s])
        for k in range(s + 1, W):
            values[k] = values[k] - lower[k, s] * out[s]
    return out

def factor_inverse(m, panel=32, between=None):
    n = m.shape[0]
    rows = [m[W * g : W * (g + 1), :] for g in range(n // W)]
    lane = lax.broadcasted_iota(jnp.int32, (W, n), 1)
    sub = lax.broadcasted_iota(jnp.int32, (W, n), 0)
    spread = lambda x: jnp.broadcast_to(x, (W, n))
    cleared = lambda x, first: jnp.where((lane >= first) & (lane < first + W), 0.0, x)
    column = lambda h, first: [spread(rows[h][:, first + s : first + s + 1]) for s in range(W)]

    def solve_rows(row, first, scale, lower):
        row = cleared(row, first)
        start = [jnp.where(lane == first + s, 1.0, spread(row[s : s + 1, :])) for s in range(W)]
        solved = forward(start, scale, lower)
        group = solved[0]
        for s in range(1, W):
            group = jnp.where(sub == s, solved[s], group)
        return solved, group

    def take(row, factors, solved, first):
        row = cleared(row, first)
        for s in range(W):
            row = row - factors[s] * solved[s]
        return row

    per = panel // W
    for p in range(n // panel):
        end = (p + 1) * per
        for q in range(0, per, 2):
            g, h = p * per + q, p * per + q + 1
            first, second = g * W, h * W
            scale, lower = pivots(column(g, first))
            cross = forward(column(h, first), scale, lower)
            crossed = {(k, s): spread(cross[s][k : k + 1, :]) for s in range(W) for k in range(W)}
            corner = column(h, second)
            for t in range(W):
                for s in range(W):
                    corner[t] = corner[t] - cross[s] * crossed[t, s]
            scale2, lower2 = pivots(corner)
            others = range(h + 1, end)
            left = {i: column(i, first) for i in others}
            right = {i: column(i, second) for i in others}
            solved, group = solve_rows(rows[g], first, scale, lower)
            rows[g] = group
            solved2, group2 = solve_rows(take(rows[h], cross, solved, first), second, scale2, lower2)
            rows[h] = group2
            for i in others:
                one = forward(left[i], scale, lower)
                two = right[i]
                for t in range(W):
                    for s in range(W):
                        two[t] = two[t] - one[s] * crossed[t, s]
                two = forward(two, scale2, lower2)
                rows[i] = take(take(rows[i], one, solved, first), two, solved2, second)
        if end < n // W:
            if between is not None:
                between(p + 1)
            edge = end * W
            kept = lambda g: jnp.where((lane < (g + 1) * W) | (lane >= edge), rows[g], 0.0)
            done = jnp.concatenate([kept(g) for g in range(p * per, end)], axis=0)
            pair = split(done)
            term = joined(pair, pair, (0, 0))
            outside = (lane < p * panel) | (lane >= (p + 1) * panel)
            for i in range(end, n // W):
                rows[i] = jnp.where(outside, rows[i], 0.0) - term[W * i : W * (i + 1), :]
    out = jnp.concatenate(rows, axis=0)
    down = lax.broadcasted_iota(jnp.int32, (n, n), 0)
    across = lax.broadcasted_iota(jnp.int32, (n, n), 1)
    return jnp.where(down >= across, out, 0.0)


def plain(a, b, dims):
    return lax.dot_general(
        a, b, (((dims[0],), (dims[1],)), ((), ())), preferred_element_type=jnp.float32
    )


def factor(work, high, low, beside=None):
    blocks, rows, order = work.shape
    down = lax.broadcasted_iota(jnp.int32, (rows, rows), 0)
    across = lax.broadcasted_iota(jnp.int32, (rows, rows), 1)
    unit = jnp.where(down == across, 1.0, 0.0)
    column_block = lax.broadcasted_iota(jnp.int32, (rows, order), 1) // rows

    def step(j, carry):
        at = pl.ds(pl.multiple_of(j * rows, rows), rows)
        if beside is not None:
            beside(j, 0)
        between = None if beside is None else functools.partial(beside, j)
        inverse = factor_inverse(work[j, :, at], between=between)
        if beside is not None:
            beside(j, POINTS - 1)
        work[j, :, at] = unit
        solved = joined(split(inverse), split(work[j]), (1, 0))
        solved_high, solved_low = split(solved)
        high[at, :] = solved_high
        low[at, :] = solved_low
        for done in range(blocks - 1):

            @pl.when(j == done)
            def _():
                here = slice(done * rows, (done + 1) * rows)
                for i in range(done + 1, blocks):
                    cut = slice(i * rows, (i + 1) * rows)
                    left = (high[here, cut].T, low[here, cut].T)
                    work[i, :, here] = jnp.zeros((rows, rows), jnp.float32)
                    work[i] = work[i] - joined(left, (solved_high, solved_low), (1, 0))

        keep = column_block <= j
        high[at, :] = jnp.where(keep, solved_high, 0.0).astype(jnp.bfloat16)
        low[at, :] = jnp.where(keep, solved_low, 0.0).astype(jnp.bfloat16)
        return carry

    lax.fori_loop(0, blocks, step, 0)


def solve(high, low, right_high, right_low, out_high, out_low, part, blocks, turn):
    order = high.shape[0]
    rows = order // blocks
    across = slice(part * order, (part + 1) * order)
    for j in range(blocks):
        at, deep = slice(j * rows, (j + 1) * rows), (j + 1) * rows
        left = (high[at, :deep], low[at, :deep])
        at_right = (slice(None), slice(part * order, part * order + deep)) if turn else (slice(deep), across)
        dims = (1, 1) if turn else (1, 0)
        if right_low is None:
            solved = plain(left[0], right_high[at_right], dims) + plain(left[1], right_high[at_right], dims)
        else:
            solved = joined(left, (right_high[at_right], right_low[at_right]), dims)
        solved_high, solved_low = split(solved)
        out_high[at, across] = solved_high
        out_low[at, across] = solved_low


def flipped(place, bit):
    return place + bit - 2 * bit * ((place // bit) % 2)


class Spread:
    def __init__(self, size, place, view, send_sem, recv_sem, base=0, own=None):
        bits = [size >> (k + 1) for k in range(size.bit_length() - 1)]
        self.plan = [(b, 0) for b in bits]
        for k, b in enumerate(bits):
            earlier = [0]
            for e in bits[:k]:
                earlier += [m + e for m in earlier]
            self.plan += [(b, m) for m in earlier if m]
        self.source = {}
        for b, m in self.plan:
            if m:
                last = m & -m
                self.source[b, m] = self.plan.index((last, m - last))
        self.copies = []
        for k, (b, m) in enumerate(self.plan):
            held = place
            for e in bits:
                if m & e:
                    held = flipped(held, e)
            self.copies.append(
                pltpu.make_async_remote_copy(
                    src_ref=own if own is not None and m == 0 else view(held),
                    dst_ref=view(held),
                    send_sem=send_sem.at[base + k],
                    recv_sem=recv_sem.at[base + k],
                    device_id={"swath": flipped(place, b)},
                    device_id_type=MESH,
                )
            )

    def start_own(self):
        for copy, (b, m) in zip(self.copies, self.plan):
            if m == 0:
                copy.start()

    def forward(self):
        waited = set()
        for copy, item in zip(self.copies, self.plan):
            if item in self.source:
                source = self.source[item]
                if source not in waited:
                    self.copies[source].wait_recv()
                    waited.add(source)
                copy.start()

    def finish(self):
        waited = set(self.source.values())
        for k, copy in enumerate(self.copies):
            if k not in waited:
                copy.wait_recv()

    def sent(self):
        for copy in self.copies:
            copy.wait_send()


class Move:
    def __init__(self, source, target, send_sem, recv_sem, index, device, sends, receives):
        self.copy = pltpu.make_async_remote_copy(
            src_ref=source,
            dst_ref=target,
            send_sem=send_sem.at[index],
            recv_sem=recv_sem.at[index],
            device_id={"tm": device},
            device_id_type=MESH,
        )
        self.target, self.sends, self.receives = target, sends, receives

    def start(self):
        pl.when(self.sends)(self.copy.start)

    def receive(self):
        pl.when(self.receives)(self.copy.wait_recv)

        @pl.when(jnp.logical_not(self.receives))
        def _():
            self.target[...] = jnp.zeros(self.target.shape, self.target.dtype)

    def sent(self):
        pl.when(self.sends)(self.copy.wait_send)


def band_cuts(rows, count, level):
    shares = SHARES[min(level, 1)] if count == 4 else (16 // count,) * count
    sizes = [rows * share // 16 for share in shares]
    return [pl.ds(sum(sizes[:c]), size) for c, size in enumerate(sizes)]


def greet(times, size, place, me):
    barrier = pltpu.get_barrier_semaphore()
    count = jnp.int32(size - 1)
    for level in range(LEVELS):
        distance = 2**level
        for there, other in ((me >= distance, me - distance), (me + distance < times, me + distance)):

            @pl.when(there)
            def _():
                pl.semaphore_signal(barrier, inc=1, device_id={"tm": other}, device_id_type=MESH)

            count = count + there.astype(jnp.int32)
    for d in range(1, size):
        pl.semaphore_signal(
            barrier, inc=1, device_id={"swath": (place + d) % size}, device_id_type=MESH
        )
    return barrier, count


def pick(weighted, routes_ref, counts_ref, owner, slot):
    block_count = routes_ref.shape[1]
    place = jnp.int32(0)
    chosen = jnp.full((), -1, jnp.int32)
    for r in range(block_count):
        named = routes_ref[0, r] == owner
        live = r < counts_ref[0, 0]
        chosen = jnp.where(named & live & (place == slot), r, chosen)
        place = place + named.astype(jnp.int32)
    block = jnp.zeros(weighted[0].shape, jnp.float32)
    for r in range(block_count):
        block = jnp.where(chosen == r, weighted[r], block)
    return block.astype(jnp.bfloat16)


def kernel(times, size, total_slots, block_rows, design_ref, process_ref, prior_ref, routes_ref,
           counts_ref, out_diag_ref, out_coup_ref, skew, obs, proc, leaving, prior, work, high, low,
           right_high, right_low, solved_high, solved_low, parts, shares, land, terms, cross, corner,
           last_cross, last_full, last_half, first_send, first_recv, spread_send, spread_recv,
           prior_send, prior_recv, inner_send, inner_recv, term_send, term_recv, cross_send, cross_recv, share_send,
           share_recv, part_send, part_recv, relay_send, relay_recv, again_send, again_recv, last_send, last_recv):
    place, me = lax.axis_index("swath"), lax.axis_index("tm")
    rows, order = process_ref.shape
    block_count = routes_ref.shape[1]
    slot_count = block_count // 2
    reach, half = size // 2, rows // 2
    hops = size - 1
    barrier, count = greet(times, size, place, me)

    behind, ahead = me >= 1, me + 1 < times
    other = flipped(place, reach)
    spread = lambda view, k, own=None: Spread(
        size, place, view, spread_send, spread_recv, k * hops, own
    )
    inner = lambda view, k: Spread(reach, place, view, inner_send, inner_recv, k * (reach - 1))
    slots = [pl.ds(c * block_rows, block_rows) for c in range(slot_count)]
    far_move = lambda source, target, k: Move(
        source, target, first_send, first_recv, k, me + 1, ahead, behind
    )
    far_moves = [
        far_move(process_ref, proc.at[1, place], 0),
        far_move(proc.at[0, other], proc.at[1, other], 1),
    ]
    for c, cut in enumerate(slots):
        far_moves.append(far_move(leaving.at[cut], obs.at[1, place, cut], c + 2))
    near_proc = spread(lambda held: proc.at[0, held], 0, process_ref)
    near_prior = Spread(size, place, lambda held: prior.at[held], prior_send, prior_recv)
    near_obs = spread(lambda held: obs.at[0, held], 1)
    far_procs = [
        inner(lambda held: proc.at[1, held], 0),
        inner(lambda held: proc.at[1, flipped(held, reach)], 1),
    ]
    far_obs = [
        spread(lambda held, cut=cut: obs.at[1, held, cut], 2 + c) for c, cut in enumerate(slots)
    ]
    prior[place] = jnp.broadcast_to(prior_ref[...], prior.shape[1:])
    pl.semaphore_wait(barrier, count)
    far_moves[0].start()
    near_proc.start_own()
    proc[0, place] = process_ref[...]

    weighted = []
    for r in range(block_count):
        raw = design_ref[r * block_rows : (r + 1) * block_rows, :].astype(jnp.float32)
        mean_sq = jnp.mean(raw * raw, axis=-1, keepdims=True)
        weighted.append(raw * lax.rsqrt(4.0 * total_slots * (mean_sq + 1e-06)))
    for slot in range(slot_count):
        cut = slice(slot * block_rows, (slot + 1) * block_rows)
        obs[0, place, cut, :] = pick(weighted, routes_ref, counts_ref, me, slot)
    near_obs.start_own()
    for slot in range(slot_count):
        cut = slice(slot * block_rows, (slot + 1) * block_rows)
        leaving[cut, :] = pick(weighted, routes_ref, counts_ref, me + 1, slot)
        far_moves[slot + 2].start()
    near_prior.start_own()
    near_proc.forward()
    far_moves[1].start()
    far_moves[0].receive()
    far_procs[0].start_own()
    near_prior.forward()
    for c in range(slot_count):
        far_moves[c + 2].receive()
        far_obs[c].start_own()
    near_obs.forward()
    near_proc.finish()
    near_prior.finish()
    near_obs.finish()

    def gram(which, cut, b):
        total = None
        for i in range(size):
            term = lax.dot_general(
                obs[which, i, cut, b * rows : (b + 1) * rows],
                obs[which, i, cut, b * rows :],
                (((0,), (0,)), ((), ())),
                preferred_element_type=jnp.float32,
            )
            total = term if total is None else total + term
        return total

    square = (rows, rows)
    unit = lax.broadcasted_iota(jnp.int32, square, 0) == lax.broadcasted_iota(jnp.int32, square, 1)
    cuts = [slice(b * rows, (b + 1) * rows) for b in range(size)]
    for b in range(size):
        work[b, :, b * rows :] = gram(0, slice(None), b)
        work[b, :, cuts[b]] += jnp.where(unit, jnp.broadcast_to(prior[b][:1], square), 0.0)
        right_high[cuts[b], :order] = proc[0, b]
    far_moves[1].receive()
    far_procs[1].start_own()
    far_obs[0].forward()
    for one in far_procs:
        one.forward()
        one.finish()
    both = lambda a, b: proc[0, a, :, cuts[b]].astype(jnp.float32) + proc[1, a, :, cuts[b]].astype(
        jnp.float32
    )
    for b in range(size):
        right_high[cuts[b], order:] = proc[1, b]
        for q in range(size):
            if q >= b:
                work[b, :, cuts[q]] += 0.5 * (both(b, q) + both(q, b).T)
    for c in range(slot_count):
        far_obs[c].finish()
        if c + 1 < slot_count:
            far_obs[c + 1].forward()
        for b in range(size):
            work[b, :, b * rows :] += gram(1, slots[c], b)
    for s in range(size):

        @pl.when(place == s)
        def _():
            for d in range(reach):
                q = (s + d) % size
                block = work[s, :, cuts[q]] if q >= s else work[q, :, cuts[s]].T
                shares[0, s, d * rows : (d + 1) * rows] = block
            a, h = s % reach, s // reach
            shares[0, s, reach * rows :] = work[a, h * half : (h + 1) * half, cuts[a + reach]]

    bands = [band_cuts(rows, size, level) for level in range(LEVELS)]
    sending = []
    column = lambda part, b: pl.ds(pl.multiple_of(part * order + b * rows, rows), rows)
    share_cuts = [pl.ds(d * rows, rows) for d in range(reach)] + [pl.ds(reach * rows, half)]
    for level in range(LEVELS):
        distance = 2**level
        last = level == LEVELS - 1
        behind, ahead = me >= distance, me + distance < times
        if level == 0:
            factor(work, high, low)
        else:
            arrivals = parts.at[level - 1]
            below = 2 ** (level - 1)
            has_next = me + 2 * below <= times
            has_previous = me >= 2 * below

            part_spreads, relays, actions = [], [], [(POINTS - 1, pending)]
            for c in range(size):
                cut = bands[level - 1][c]
                base = ((level - 1) * size + c) * hops
                kinds = (has_next, has_previous)
                arrive = [
                    Move(cross.at[level - 1, k, cut], arrivals.at[place, k, cut], cross_send,
                         cross_recv, ((level - 1) * size + c) * 2 + k, me, kinds[k], kinds[k])
                    for k in range(2)
                ]
                if level == 1:
                    relay = Move(
                        arrivals.at[place, 0, cut], arrivals.at[place, 1, cut], relay_send, relay_recv,
                        c, me + 2 * below, me + 2 * below < times, has_previous,
                    )
                    pair_of = [
                        Spread(size, place, lambda held, cut=cut, k=k: arrivals.at[held, k, cut],
                               sems[0], sems[1], first)
                        for k, sems, first in (
                            (0, (part_send, part_recv), base),
                            (1, (again_send, again_recv), c * hops),
                        )
                    ]

                    def landed(arrive=arrive, relay=relay, pair_of=pair_of):
                        arrive[0].receive()
                        relay.start()
                        pair_of[0].start_own()

                    def relayed(relay=relay, pair_of=pair_of):
                        relay.receive()
                        pair_of[1].start_own()

                    steps = (landed, pair_of[0].forward, relayed, pair_of[1].forward)
                    relays.append(relay)
                else:
                    pair_of = [
                        Spread(size, place, lambda held, cut=cut: arrivals.at[held, :, cut], part_send,
                               part_recv, base)
                    ]

                    def landed(arrive=arrive, pair_of=pair_of):
                        for move in arrive:
                            move.receive()
                        pair_of[0].start_own()

                    steps = (landed, pair_of[0].forward)
                part_spreads += pair_of
                actions += list(zip(PLAN[min(level, 2) - 1][c % 4], steps))
            actions.sort(key=lambda item: item[0])

            def beside(j, spot):
                for point, act in actions:
                    if point % POINTS == spot and point < POINTS * size:
                        pl.when(j == point // POINTS)(act)

            factor(work, high, low, beside)
            for point, act in actions:
                if point >= POINTS * size:
                    act()
            for one in part_spreads:
                one.finish()
            sending += part_spreads + relays
            for b in range(size):
                for part in range(2):
                    top, bottom = split(arrivals[b, part])
                    right_high[cuts[b], part * order : (part + 1) * order] = top
                    right_low[cuts[b], part * order : (part + 1) * order] = bottom

        goes_down = behind & (me + distance <= times)
        comes_down = me + 2 * distance <= times
        whole = lambda part: (
            solved_high[:, part * order : (part + 1) * order],
            solved_low[:, part * order : (part + 1) * order],
        )
        lower = None if level == 0 else right_low
        term_moves, turned = [None, None], [None, None]
        for part in (1, 0) if last else (0, 1):
            turn = part == 1 and level < 2
            solve(high, low, right_high, lower, solved_high, solved_low, part, size, turn)
            pair = lambda b, part=part: (solved_high[:, column(part, b)], solved_low[:, column(part, b)])
            own = pair(place)
            own = (own[0].T, own[1].T)
            turned[part] = own
            if last and part == 0:
                cross[level, 0] = joined(turned[1], whole(0), (1, 0))
                final = Move(
                    cross.at[level, 0], last_cross, last_send, last_recv, 0, me - distance, goes_down,
                    comes_down,
                )
                final.start()
            wide = [pair((place + d) % size) for d in range(reach)]
            wide = tuple(jnp.concatenate([w[k] for w in wide], axis=1) for k in range(2))
            product = joined(own, wide, (1, 0))
            for d in range(reach):
                terms[level, part, d * rows : (d + 1) * rows] = product[:, d * rows : (d + 1) * rows]
            a, h = place % reach, place // reach
            first = pair(a)
            corner[...] = joined((first[0].T, first[1].T), pair(a + reach), (1, 0))
            terms[level, part, reach * rows :] = corner[pl.ds(pl.multiple_of(h * half, half), half), :]
            sends, receives = (ahead, behind) if part == 0 else (behind, ahead)
            moves = []
            for d, cut in enumerate(share_cuts):
                move = Move(
                    terms.at[level, part, cut], land.at[level, part, cut], term_send, term_recv,
                    (level * 2 + part) * len(share_cuts) + d,
                    me + distance if part == 0 else me - distance, sends, receives,
                )
                moves.append(move)
            moves[0].start()
            if last:
                for move in moves[1:]:
                    move.start()
            term_moves[part] = moves

        if not last:
            for d in range(1, len(share_cuts)):
                for part in range(2):
                    term_moves[part][d].start()

        cross_moves = []
        if not last:
            cross[level, 0] = joined(turned[1], whole(0), (1, 0))
            if level > 0:
                cross[level, 1] = joined(turned[0], whole(1), (1, 0))
            target = parts.at[level]
            for c in range(size):
                cut = bands[level][c]
                index = (level * size + c) * 2
                cross_moves.append(
                    Move(cross.at[level, 0, cut], target.at[place, 0, cut], cross_send, cross_recv,
                         index, me - distance, goes_down, comes_down)
                )
                if level == 0:
                    continue
                cross_moves.append(
                    Move(cross.at[level, 1, cut], target.at[place, 1, cut], cross_send, cross_recv,
                         index + 1, me + distance, behind & ahead, me >= 2 * distance)
                )
            for move in cross_moves:
                move.start()

        spreads = []
        for d, cut in enumerate(share_cuts):
            term_moves[0][d].receive()
            term_moves[1][d].receive()
            shares[level + 1, place, cut] = (
                shares[level, place, cut] - land[level, 0, cut] - land[level, 1, cut]
            )
            if not last:
                spreads.append(
                    Spread(size, place, lambda held, cut=cut: shares.at[level + 1, held, cut],
                           share_send, share_recv, (level * len(share_cuts) + d) * hops)
                )
                spreads[-1].start_own()
                if d == len(share_cuts) - 2:
                    spreads[0].forward()
        sending += term_moves[0] + term_moves[1] + cross_moves + spreads
        if level == 0:
            mine = pl.ds(pl.multiple_of(place * rows, rows), rows)
            for q in range(size):
                there = proc[0, q, :, mine].astype(jnp.float32) + proc[1, q, :, mine].astype(jnp.float32)
                here = proc[0, place, :, cuts[q]].astype(jnp.float32) + proc[
                    1, place, :, cuts[q]
                ].astype(jnp.float32)
                skew[:, cuts[q]] = 0.5 * (here - there.T)
        if not last:
            spreads[0].finish()
            held = shares.at[level + 1]
            for s in range(size):
                work[s, :, cuts[s]] = held[s, :rows]

            def pending(spreads=spreads, held=held):
                for one in spreads[1:]:
                    one.forward()
                for one in spreads[1:]:
                    one.finish()
                for s in range(size):
                    for d in range(1, reach):
                        q = (s + d) % size
                        block = held[s, d * rows : (d + 1) * rows]
                        if q >= s:
                            work[s, :, cuts[q]] = block
                        else:
                            work[q, :, cuts[s]] = block.T
                    a, h = s % reach, s // reach
                    work[a, h * half : (h + 1) * half, cuts[a + reach]] = held[s, reach * rows :]

    copies = []
    for d in range(1, reach):
        copies.append(
            pltpu.make_async_remote_copy(
                src_ref=shares.at[LEVELS, place, share_cuts[d]],
                dst_ref=last_full.at[d - 1],
                send_sem=last_send.at[d],
                recv_sem=last_recv.at[d],
                device_id={"swath": (place + d) % size},
                device_id_type=MESH,
            )
        )
    copies.append(
        pltpu.make_async_remote_copy(
            src_ref=shares.at[LEVELS, place, share_cuts[reach]],
            dst_ref=last_half,
            send_sem=last_send.at[reach],
            recv_sem=last_recv.at[reach],
            device_id={"swath": (place + reach) % size},
            device_id_type=MESH,
        )
    )
    for copy in copies:
        copy.start()
    final.receive()
    out_coup_ref[...] = last_cross[...]
    for copy in copies:
        copy.wait_recv()
    for s in range(size):

        @pl.when(place == s)
        def _():
            own = shares.at[LEVELS, s]
            for d in range(reach):
                q = (s + d) % size
                out_diag_ref[:, cuts[q]] = own[d * rows : (d + 1) * rows]
            for d in range(1, reach):
                q = (s - d) % size
                out_diag_ref[:, cuts[q]] = last_full[d - 1].T
            pieces = [own[reach * rows :], last_half[...]]
            if s < reach:
                block = jnp.concatenate(pieces, axis=0)
            else:
                block = jnp.concatenate(pieces[::-1], axis=0).T
            q = (s + reach) % size
            out_diag_ref[:, cuts[q]] = block

    for copy in copies:
        copy.wait_send()
    final.sent()
    for move in far_moves + sending:
        move.sent()
    for one in [near_proc, near_prior, near_obs] + far_procs + far_obs:
        one.sent()


def shards(design, process, prior_prec, routes, counts):
    times, size = lax.axis_size("tm"), lax.axis_size("swath")
    rows, order = process.shape[1:]
    block_count = routes.shape[1]
    block_rows = design.shape[1] // block_count
    slot_count = block_count // 2
    observed = slot_count * block_rows
    total_slots = 2 * observed * size
    share = rows * (size // 2) + rows // 2
    hops = size - 1
    kinds = size // 2 + 1
    vmem, smem = (pl.BlockSpec(memory_space=m) for m in (pltpu.VMEM, pltpu.SMEM))
    f32, bf16 = jnp.float32, jnp.bfloat16
    dma = lambda n: [pltpu.SemaphoreType.DMA((n,))] * 2
    diag_rows, coup_rows, skew = pl.pallas_call(
        functools.partial(kernel, times, size, total_slots, block_rows),
        out_shape=(jax.ShapeDtypeStruct((rows, order), f32),) * 3,
        in_specs=[vmem, vmem, vmem, smem, smem],
        out_specs=(vmem,) * 3,
        scratch_shapes=[
            pltpu.VMEM((2, size, observed, order), bf16),
            pltpu.VMEM((2, size, rows, order), bf16),
            pltpu.VMEM((observed, order), bf16),
            pltpu.VMEM((size, 8, rows), f32),
            pltpu.VMEM((size, rows, order), f32),
            pltpu.VMEM((order, order), bf16),
            pltpu.VMEM((order, order), bf16),
            pltpu.VMEM((order, 2 * order), bf16),
            pltpu.VMEM((order, 2 * order), bf16),
            pltpu.VMEM((order, 2 * order), bf16),
            pltpu.VMEM((order, 2 * order), bf16),
            pltpu.VMEM((LEVELS - 1, size, 2, rows, order), f32),
            pltpu.VMEM((LEVELS + 1, size, share, rows), f32),
            pltpu.VMEM((LEVELS, 2, share, rows), f32),
            pltpu.VMEM((LEVELS, 2, share, rows), f32),
            pltpu.VMEM((LEVELS, 2, rows, order), f32),
            pltpu.VMEM((rows, rows), f32),
            pltpu.VMEM((rows, order), f32),
            pltpu.VMEM((max(size // 2 - 1, 1), rows, rows), f32),
            pltpu.VMEM((rows // 2, rows), f32),
        ]
        + dma(2 + slot_count)
        + dma((2 + slot_count) * hops)
        + dma(hops)
        + dma(2 * (size // 2 - 1))
        + dma(LEVELS * 2 * kinds)
        + dma((LEVELS - 1) * size * 2)
        + dma((LEVELS - 1) * kinds * hops)
        + dma((LEVELS - 1) * size * hops)
        + dma(size)
        + dma(size * hops)
        + dma(kinds),
        compiler_params=pltpu.CompilerParams(collective_id=0, has_side_effects=True),
    )(design[0], process[0], prior_prec, routes, counts)
    return ((diag_rows + skew)[None], -coup_rows[None])


def solution(mesh):
    return jax.shard_map(
        shards,
        mesh=mesh,
        in_specs=(
            P("tm", "swath", None),
            P("tm", "swath", None),
            P("tm", "swath"),
            P("tm", "swath"),
            P("tm", "swath"),
        ),
        out_specs=(P("tm", "swath", None), P("tm", "swath", None)),
        check_vma=False,
    )
```
